256 devices in a mesh: user: 16 (over y, x_hi, core), item: 16 (over z, x_lo).
Axes of the slice: x: 4 (x_hi: 2, x_lo: 2; x = x_hi * 2 + x_lo), y: 4, z: 8, core: 2. Of those that a mesh axis runs over, the one named last changes fastest.
Arguments:
- ratings: bfloat16 [12288, 24576], P('user', 'item')
- presence: int32 [96, 192], P('user', 'item'), may hold values from 0 to 1
- user_factors: float32 [12288, 128], P('user'), may hold values from -4 to 4
- item_factors: float32 [24576, 128], P('item'), may hold values from -4 to 4
- step_sizes: float32 [2], replicated, may hold values from 0.3 to 0.7
Outputs:
- new_users: float32 [12288, 128], P('user')
- new_items: float32 [24576, 128], P('item')
The draws below stay inside these ranges and needn't reach their ends.
All inputs are finite; a program needn't handle non-finite values.
Results may differ from the reference program's by a relative error of at most 0.0003.
Values sent between devices are 32-bit elements; how exact they have to be, the bound alone decides.
No kernel may reach another device: no remote copies, remote signals or barrier semaphores. Data moves between devices by JAX's collectives and lax.ppermute only.
A program may use at most 64 MiB of HBM per device.

```python
import jax
import jax.numpy as jnp
from jax import lax

K = 128
BLK = 128
USERS = 12288
ITEMS = 24576
UBLK = 96
IBLK = 192


def draw_presence(key, part):
    first, second, third = jax.random.split(jax.random.fold_in(key, 11), 3)
    row_level = jax.random.randint(first, (UBLK, 1), 1, 9)
    col_level = jax.random.randint(second, (1, IBLK), 0, 8)
    rolled = jax.random.randint(third, (UBLK, IBLK), 0, 16)
    return (rolled < row_level + col_level).astype(jnp.int32)


def draw_ratings(key, part):
    first = jax.random.fold_in(jax.random.fold_in(key, 23), 0)
    spread = 0.5 * jnp.sqrt(jnp.float32(ITEMS) / 2.0)
    values = jnp.clip(jax.random.normal(first, (USERS, ITEMS), jnp.float32), -6.0, 6.0) * spread
    return values.astype(jnp.bfloat16)


def levels(rng, dims, pieces, smallest, largest):
    level = 1.0
    for dim, parts in pieces:
        heights = jax.random.uniform(jax.random.fold_in(jax.random.fold_in(rng, 6), dim), (parts,), jnp.float32, smallest / len(pieces), largest / len(pieces))
        level = level * jnp.repeat(jnp.exp(heights), dims[dim] // parts).reshape((-1,) + (1,) * (len(dims) - 1 - dim))
    return level


def noise(own_key, extent, width, reach, cuts=(), dtype=jnp.bfloat16):
    values = jax.random.normal(own_key, extent, jnp.float32) * width
    if len(cuts) > 0:
        values = levels(own_key, extent, cuts, -0.22, 0.18) * values
    return jnp.clip(values, min=-reach, max=reach).astype(dtype)


def setup_inputs(seed: int = 0) -> dict:
    arg_keys = jax.random.split(jax.random.key(seed), 6)
    return {
        "ratings": draw_ratings(jax.random.fold_in(arg_keys[5], 71), 0),
        "presence": draw_presence(jax.random.fold_in(arg_keys[5], 71), 0),
        "user_factors": noise(arg_keys[2], (USERS, K), 1.0, 4.0, ((0, 16),), jnp.float32),
        "item_factors": noise(arg_keys[3], (ITEMS, K), 1.0, 4.0, ((0, 16),), jnp.float32),
        "step_sizes": jnp.clip(jax.random.uniform(arg_keys[4], (2,), jnp.float32, 0.3, 0.7), 0.3, 0.7),
    }


highest = lax.Precision.HIGHEST

def block_residual(rating_rows, mask_row, user_rows, item_factors):
    predicted = jnp.dot(user_rows, item_factors.T, precision=highest, preferred_element_type=jnp.float32)
    present = jnp.repeat(mask_row.astype(jnp.float32), BLK)
    return (rating_rows.astype(jnp.float32) - predicted) * present[None, :]

def reference(ratings, presence, user_factors, item_factors, step_sizes):
    user_blocks = USERS // BLK
    rating_blocks = ratings.reshape(user_blocks, BLK, ITEMS)
    users = user_factors.reshape(user_blocks, BLK, K)
    user_scale = step_sizes[0] / (BLK * (1.0 + lax.optimization_barrier(jnp.sum(presence, axis=1)).astype(jnp.float32)))
    item_scale = step_sizes[1] / (BLK * (1.0 + lax.optimization_barrier(jnp.sum(presence, axis=0)).astype(jnp.float32)))
    item_scale = jnp.repeat(item_scale, BLK)

    def user_grad(packed):
        rating_rows, mask_row, user_rows = packed
        resid = block_residual(rating_rows, mask_row, user_rows, item_factors)
        return jnp.dot(resid, item_factors, precision=highest, preferred_element_type=jnp.float32)
    for sweep in range(2):
        gradients = lax.map(user_grad, (rating_blocks, presence, users))
        users = users + gradients * user_scale[:, None, None]

    def add_block(running, packed):
        rating_rows, mask_row, user_rows = packed
        resid = block_residual(rating_rows, mask_row, user_rows, item_factors)
        return (running + jnp.dot(resid.T, user_rows, precision=highest, preferred_element_type=jnp.float32), None)
    summed, _ = lax.scan(add_block, jnp.zeros((ITEMS, K), jnp.float32), (rating_blocks, presence, users))
    new_items = item_factors + summed * item_scale[:, None]
    return (users.reshape(USERS, K), new_items)
```

```python
import jax
import jax.numpy as jnp
from jax import lax
from jax.experimental import pallas as pl
from jax.experimental.pallas import tpu as pltpu
from jax.sharding import PartitionSpec as P

BLK = 128
UB = 6
IB = 12
USERS = UB * BLK
ITEMS = IB * BLK
PIECES = 16
ROWS = USERS // PIECES
HROWS = UB * 64 // PIECES
PIECE = ROWS + HROWS + 8
CHUNK = ITEMS // 16
F32 = jnp.float32
BF16 = jnp.bfloat16
VMEM = pl.BlockSpec(memory_space=pltpu.VMEM)
SMEM = pl.BlockSpec(memory_space=pltpu.SMEM)
ANY = pl.BlockSpec(memory_space=pl.ANY)


def split(value):
    high = value.astype(BF16)
    low = (value - high.astype(F32)).astype(BF16)
    return jnp.concatenate([high, low], axis=1)


def gram(both):
    square = lax.dot_general(both, both, (((0,), (0,)), ((), ())), preferred_element_type=F32)
    return (square[:BLK, :BLK] + square[BLK:, BLK:]) + (square[:BLK, BLK:] + square[BLK:, :BLK])


def exact(a, b, dims):
    return lax.dot_general(a, b, (dims, ((), ())), precision=lax.Precision.HIGHEST, preferred_element_type=F32)


def lanes(shape):
    return lax.broadcasted_iota(jnp.int32, shape, 1)


def sublanes(shape):
    return lax.broadcasted_iota(jnp.int32, shape, 0)


def fetch_ratings(r_hbm, r_vmem, sem):
    copies = []
    for b in range(UB):
        rows = pl.ds(b * BLK, BLK)
        copies.append(pltpu.make_async_copy(r_hbm.at[rows], r_vmem.at[rows], sem.at[b]))
        copies[-1].start()
    return copies


def user_kernel(m_ref, r_hbm, p_ref, q_ref, x_ref, r_vmem, qcat, grams, packed, sem):
    copies = fetch_ratings(r_hbm, r_vmem, sem)
    for j in range(IB):
        rows = slice(j * BLK, (j + 1) * BLK)
        both = split(q_ref[rows])
        qcat[rows] = both
        grams[j] = gram(both)
    row64, lane64 = sublanes((64, BLK)), lanes((64, BLK))
    extra_row = sublanes((8, BLK))
    extra_lane = lanes((8, BLK))
    extra = jnp.zeros((8, BLK), F32)
    for b in range(UB):
        h = jnp.zeros((BLK, BLK), F32)
        count = jnp.int32(0)
        for j in range(IB):
            h = h + m_ref[b, j].astype(F32) * grams[j]
            count = count + m_ref[b, j]
        turned = jnp.concatenate([h[64:, 64:], h[64:, :64]], axis=1)
        packed[b * 64 : (b + 1) * 64] = jnp.where((lane64 < 64) & (lane64 > row64), turned, h[:64])
        diagonal = jnp.sum(jnp.where(lane64 == row64 + 64, h[64:], 0.0), axis=0, keepdims=True)
        extra = extra + jnp.where(extra_row == b, jnp.broadcast_to(diagonal, (8, BLK)), 0.0)
        extra = extra + jnp.where((extra_row == 6) & (extra_lane == b), count.astype(F32), 0.0)
        copies[b].wait()
        rows = slice(b * BLK, (b + 1) * BLK)
        masked = jnp.concatenate(
            [r_vmem[rows, j * BLK : (j + 1) * BLK] * m_ref[b, j].astype(F32).astype(BF16) for j in range(IB)],
            axis=1,
        )
        found = jnp.dot(masked, qcat[...], preferred_element_type=F32)
        d = found[:, :BLK] + found[:, BLK:] - exact(p_ref[rows], h, ((1,), (0,)))
        for k in range(0, BLK, 16):
            piece, at = divmod(b * BLK + k, ROWS)
            x_ref[piece, at : at + 16] = d[k : k + 16]
    for piece in range(PIECES):
        x_ref[piece, ROWS : ROWS + HROWS] = packed[piece * HROWS : (piece + 1) * HROWS]
        x_ref[piece, ROWS + HROWS :] = extra if piece == 0 else jnp.zeros((8, BLK), F32)


def total_kernel(y_ref, z_ref):
    total = y_ref[0]
    for k in range(1, PIECES):
        total = total + y_ref[k]
    for k in range(PIECES):
        z_ref[k] = total


def item_kernel(
    m_ref, step_ref, core_ref, r_hbm, p_ref, q_ref, z_ref, new_ref, own_ref, other_ref, r_vmem, pcat, grams, grads, sem
):
    copies = fetch_ratings(r_hbm, r_vmem, sem)
    extra = z_ref[0, ROWS + HROWS :]
    scales = step_ref[0] / (BLK * (1.0 + extra[6:7]))
    row64, lane64 = sublanes((64, BLK)), lanes((64, BLK))
    for b in range(UB):
        rows = slice(b * BLK, (b + 1) * BLK)
        tiles = []
        for k in range(0, BLK, 16):
            piece, at = divmod(b * BLK + k, ROWS)
            tiles.append(z_ref[piece, at : at + 16])
        d = jnp.concatenate(tiles, axis=0)
        tiles = []
        for k in range(0, 64, 8):
            piece, at = divmod(b * 64 + k, HROWS)
            tiles.append(z_ref[piece, ROWS + at : ROWS + at + 8])
        half = jnp.concatenate(tiles, axis=0)
        turned = jnp.concatenate([half[:, 64:], half[:, :64]], axis=1)
        top = jnp.where(lane64 < row64, half, jnp.where(lane64 == row64, 0.5 * half, 0.0))
        top = jnp.where(lane64 >= 64, half, top)
        bottom = jnp.where(lane64 > row64 + 64, turned, 0.0)
        bottom = jnp.where(lane64 == row64 + 64, 0.5 * extra[b : b + 1], bottom)
        w = jnp.concatenate([top, bottom], axis=0)
        dh = exact(d, w, ((1,), (0,))) + exact(d, w, ((1,), (1,)))
        s = scales[:, b : b + 1]
        new = p_ref[rows] + (2.0 * s) * d - (s * s) * dh
        new_ref[rows] = new
        both = split(new)
        pcat[rows] = both
        grams[b] = gram(both)
    for b in range(UB):
        copies[b].wait()
        rows = slice(b * BLK, (b + 1) * BLK)
        for j in range(IB):
            columns = slice(j * BLK, (j + 1) * BLK)
            r_vmem[rows, columns] = r_vmem[rows, columns] * m_ref[b, j].astype(F32).astype(BF16)
    counts = jnp.zeros((8, BLK), F32)
    lane8 = lanes((8, BLK))
    for j in range(IB):
        columns = slice(j * BLK, (j + 1) * BLK)
        s = jnp.zeros((BLK, BLK), F32)
        count = jnp.int32(0)
        for b in range(UB):
            s = s + m_ref[b, j].astype(F32) * grams[b]
            count = count + m_ref[b, j]
        counts = counts + jnp.where(lane8 == j, count.astype(F32), 0.0)
        found = lax.dot_general(
            pcat[...], r_vmem[:, columns], (((0,), (0,)), ((), ())), preferred_element_type=F32
        )
        grads[columns] = (found[:BLK] + found[BLK:]).T - exact(q_ref[columns], s, ((1,), (0,)))
    core = core_ref[0]
    for k in range(8):
        own_ref[k, :CHUNK] = grads[pl.ds(pl.multiple_of(k * 2 * CHUNK + core * CHUNK, 8), CHUNK)]
        other_ref[k, :CHUNK] = grads[pl.ds(pl.multiple_of(k * 2 * CHUNK + (1 - core) * CHUNK, 8), CHUNK)]
        own_ref[k, CHUNK:] = counts
        other_ref[k, CHUNK:] = counts


def scale_kernel(step_ref, user_ref, v_ref, q_ref, o_ref):
    total = v_ref[0]
    for k in range(1, 8):
        total = total + v_ref[k]
    scales = step_ref[1] / (BLK * (1.0 + total[CHUNK : CHUNK + 1]))
    lane1 = lanes((1, BLK))
    for k in range(3):
        block = (user_ref[0] * 3 + k) // 4
        t = jnp.sum(jnp.where(lane1 == block, scales, 0.0), axis=1, keepdims=True)
        start = pl.multiple_of(user_ref[0] * CHUNK + k * 32, 8)
        o_ref[k * 32 : (k + 1) * 32] = q_ref[pl.ds(start, 32)] + t * total[k * 32 : (k + 1) * 32]


def spread_kernel(core_ref, own_ref, other_ref, o_ref):
    core = core_ref[0]
    for k in range(8):
        o_ref[k, pl.ds(pl.multiple_of(core * CHUNK, 8), CHUNK)] = own_ref[...]
        o_ref[k, pl.ds(pl.multiple_of((1 - core) * CHUNK, 8), CHUNK)] = other_ref[...]


def call(kernel, out_shapes, specs, scratch=(), single=True):
    shapes = [jax.ShapeDtypeStruct(s, F32) for s in out_shapes]
    return pl.pallas_call(
        kernel,
        out_shape=shapes[0] if single else shapes,
        in_specs=specs,
        out_specs=VMEM if single else [VMEM] * len(shapes),
        scratch_shapes=scratch,
    )


def body(ratings, presence, user_factors, item_factors, step_sizes):
    user = lax.axis_index("user")
    core = lax.rem(user, 2)
    user1, core1 = user.reshape(1), core.reshape(1)
    swap = [(k, k ^ 1) for k in range(16)]
    chips = [[k + 2 * j for j in range(8)] for k in range(2)]
    x = call(
        user_kernel,
        [(PIECES, PIECE, BLK)],
        [SMEM, ANY, VMEM, VMEM],
        [
            pltpu.VMEM((USERS, ITEMS), BF16),
            pltpu.VMEM((ITEMS, 2 * BLK), BF16),
            pltpu.VMEM((IB, BLK, BLK), F32),
            pltpu.VMEM((UB * 64, BLK), F32),
            pltpu.SemaphoreType.DMA((UB,)),
        ],
    )(presence, ratings, user_factors, item_factors)
    y = lax.all_to_all(x, "item", 0, 0, tiled=True)
    z = call(total_kernel, [(PIECES, PIECE, BLK)], [VMEM])(y)
    z = lax.all_to_all(z, "item", 0, 0, tiled=True)
    new_users, own, other = call(
        item_kernel,
        [(USERS, BLK), (8, CHUNK + 8, BLK), (8, CHUNK + 8, BLK)],
        [SMEM, SMEM, SMEM, ANY, VMEM, VMEM, VMEM],
        [
            pltpu.VMEM((USERS, ITEMS), BF16),
            pltpu.VMEM((USERS, 2 * BLK), BF16),
            pltpu.VMEM((UB, BLK, BLK), F32),
            pltpu.VMEM((ITEMS, BLK), F32),
            pltpu.SemaphoreType.DMA((UB,)),
        ],
        single=False,
    )(presence, step_sizes, core1, ratings, user_factors, item_factors, z)
    v = own + lax.ppermute(other, "user", swap)
    v = lax.all_to_all(v, "user", 0, 0, tiled=True, axis_index_groups=chips)
    owned = call(scale_kernel, [(CHUNK, BLK)], [SMEM, SMEM, VMEM, VMEM])(step_sizes, user1, v, item_factors)
    partner = lax.ppermute(owned, "user", swap)
    w = call(spread_kernel, [(8, 2 * CHUNK, BLK)], [SMEM, VMEM, VMEM])(core1, owned, partner)
    w = lax.all_to_all(w, "user", 0, 0, tiled=True, axis_index_groups=chips)
    return new_users, w.reshape(ITEMS, BLK)


def solution(mesh):
    return jax.shard_map(
        body,
        mesh=mesh,
        in_specs=(P("user", "item"), P("user", "item"), P("user", None), P("item", None), P()),
        out_specs=(P("user", None), P("item", None)),
        check_vma=False,
    )
```

```python
import jax
import jax.numpy as jnp
from jax import lax
from jax.experimental import pallas as pl
from jax.experimental.pallas import tpu as pltpu
from jax.sharding import PartitionSpec as P

BLK = 128
UB = 6
IB = 12
USERS = UB * BLK
ITEMS = IB * BLK
PIECES = 16
ROWS = USERS // PIECES
HROWS = UB * 64 // PIECES
PIECE = ROWS + HROWS + 8
CHUNK = ITEMS // 16
F32 = jnp.float32
BF16 = jnp.bfloat16
VMEM = pl.BlockSpec(memory_space=pltpu.VMEM)
SMEM = pl.BlockSpec(memory_space=pltpu.SMEM)
HBM = pl.BlockSpec(memory_space=pltpu.HBM)


def split(value, axis):
    high = value.astype(BF16)
    low = (value - high.astype(F32)).astype(BF16)
    return jnp.concatenate([high, low], axis=axis)


def halves(value):
    return value[:, :BLK] + value[:, BLK:]


def gram(both, turned):
    square = jnp.dot(turned, both, preferred_element_type=F32)
    return halves(square[:BLK] + square[BLK:])


def thirds(value):
    high = value.astype(BF16)
    rest = value - high.astype(F32)
    middle = rest.astype(BF16)
    return high, middle, (rest - middle.astype(F32)).astype(BF16)


def exact(a, b):
    ah, am, al = thirds(a)
    bh, bm, bl = thirds(b)
    left = jnp.concatenate([ah, am, ah, al], axis=1)
    near_zero = jnp.zeros_like(bl)
    right = jnp.concatenate(
        [
            jnp.concatenate([bh, bh, bl, bh], axis=0),
            jnp.concatenate([bm, bm, near_zero, near_zero], axis=0),
        ],
        axis=1,
    )
    return halves(jnp.dot(left, right, preferred_element_type=F32))


def lanes(shape):
    return lax.broadcasted_iota(jnp.int32, shape, 1)


def sublanes(shape):
    return lax.broadcasted_iota(jnp.int32, shape, 0)


def block(index):
    return slice(index * BLK, (index + 1) * BLK)


def present(m_ref, b, j):
    return m_ref[b, j].astype(F32)


def fetch_ratings(r_hbm, r_ref, sem):
    copies = []
    for b in range(UB):
        rows = pl.ds(b * BLK, BLK)
        copies.append(pltpu.make_async_copy(r_hbm.at[rows], r_ref.at[rows], sem.at[b]))
        copies[-1].start()
    return copies


def keep_present(m_ref, r_ref, b):
    for j in range(IB):
        r_ref[block(b), block(j)] = r_ref[block(b), block(j)] * present(m_ref, b, j).astype(BF16)


def user_kernel(m_ref, r_hbm, p_hbm, q_hbm, x_ref, r_ref, p_ref, q_ref, qcat, grams, packed, r_sem, q_sem, p_sem):
    q_copies = []
    for k in range(4):
        rows = pl.ds(k * 3 * BLK, 3 * BLK)
        q_copies.append(pltpu.make_async_copy(q_hbm.at[rows], q_ref.at[rows], q_sem.at[k]))
        q_copies[-1].start()
    r_copies = fetch_ratings(r_hbm, r_ref, r_sem)
    p_copy = pltpu.make_async_copy(p_hbm, p_ref, p_sem)
    p_copy.start()
    for j in range(IB):
        if j % 3 == 0:
            q_copies[j // 3].wait()
        q = q_ref[block(j)]
        both = split(q, 1)
        qcat[block(j)] = both
        grams[j] = gram(both, split(q.T, 0))
    row64, lane64 = sublanes((64, BLK)), lanes((64, BLK))
    extra_row, extra_lane = sublanes((8, BLK)), lanes((8, BLK))
    extra = jnp.zeros((8, BLK), F32)
    p_copy.wait()
    for half in range(2):
        three = range(half * 3, half * 3 + 3)
        corrections = []
        for b in three:
            h = jnp.zeros((BLK, BLK), F32)
            count = jnp.int32(0)
            for j in range(IB):
                h = h + present(m_ref, b, j) * grams[j]
                count = count + m_ref[b, j]
            turned = jnp.concatenate([h[64:, 64:], h[64:, :64]], axis=1)
            packed[b * 64 : (b + 1) * 64] = jnp.where((lane64 < 64) & (lane64 > row64), turned, h[:64])
            diagonal = jnp.sum(jnp.where(lane64 == row64 + 64, h[64:], 0.0), axis=0, keepdims=True)
            extra = extra + jnp.where(extra_row == b, jnp.broadcast_to(diagonal, (8, BLK)), 0.0)
            extra = extra + jnp.where((extra_row == 6) & (extra_lane == b), count.astype(F32), 0.0)
            corrections.append(exact(p_ref[block(b)], h))
            r_copies[b].wait()
            keep_present(m_ref, r_ref, b)
        found = halves(
            jnp.dot(r_ref[half * 3 * BLK : (half + 1) * 3 * BLK], qcat[...], preferred_element_type=F32)
        )
        d = found - jnp.concatenate(corrections, axis=0)
        for k in range(8):
            x_ref[half * 8 + k, :ROWS] = d[k * ROWS : (k + 1) * ROWS]
    for piece in range(PIECES):
        x_ref[piece, ROWS : ROWS + HROWS] = packed[piece * HROWS : (piece + 1) * HROWS]
        x_ref[piece, ROWS + HROWS :] = extra if piece == 0 else jnp.zeros((8, BLK), F32)


def total_kernel(y_ref, z_ref):
    total = y_ref[0]
    for k in range(1, PIECES):
        total = total + y_ref[k]
    for k in range(PIECES):
        z_ref[k] = total


def item_kernel(
    m_ref, step_ref, core_ref, r_hbm, p_ref, q_ref, z_ref, new_ref, own_ref, other_ref, r_ref, turned_ref, grams, grads, sem
):
    copies = fetch_ratings(r_hbm, r_ref, sem)
    extra = z_ref[0, ROWS + HROWS :]
    scales = step_ref[0] / (BLK * (1.0 + extra[6:7]))
    row64, lane64 = sublanes((64, BLK)), lanes((64, BLK))
    for b in range(UB):
        tiles = []
        for k in range(0, BLK, 16):
            piece, at = divmod(b * BLK + k, ROWS)
            tiles.append(z_ref[piece, at : at + 16])
        d = jnp.concatenate(tiles, axis=0)
        tiles = []
        for k in range(0, 64, 8):
            piece, at = divmod(b * 64 + k, HROWS)
            tiles.append(z_ref[piece, ROWS + at : ROWS + at + 8])
        half = jnp.concatenate(tiles, axis=0)
        turned = jnp.concatenate([half[:, 64:], half[:, :64]], axis=1)
        top = jnp.where(lane64 < row64, half, jnp.where(lane64 == row64, 0.5 * half, 0.0))
        top = jnp.where(lane64 >= 64, half, top)
        bottom = jnp.where(lane64 > row64 + 64, turned, 0.0)
        bottom = jnp.where(lane64 == row64 + 64, 0.5 * extra[b : b + 1], bottom)
        w = jnp.concatenate([top, bottom], axis=0)
        s = scales[:, b : b + 1]
        new = p_ref[block(b)] + (2.0 * s) * d - (s * s) * exact(d, w + w.T)
        new_ref[block(b)] = new
        turned = split(new.T, 0)
        turned_ref[:, block(b)] = turned
        grams[b] = gram(split(new, 1), turned)
        copies[b].wait()
        keep_present(m_ref, r_ref, b)
    counts = jnp.zeros((8, BLK), F32)
    lane8 = lanes((8, BLK))
    for pair in range(IB // 2):
        found = jnp.dot(
            turned_ref[...], r_ref[:, pair * 2 * BLK : (pair + 1) * 2 * BLK], preferred_element_type=F32
        )
        found = found[:BLK] + found[BLK:]
        for k in range(2):
            j = pair * 2 + k
            s = jnp.zeros((BLK, BLK), F32)
            count = jnp.int32(0)
            for b in range(UB):
                s = s + present(m_ref, b, j) * grams[b]
                count = count + m_ref[b, j]
            counts = counts + jnp.where(lane8 == j, count.astype(F32), 0.0)
            grads[block(j)] = found[:, block(k)].T - exact(q_ref[block(j)], s)
    core = core_ref[0]
    for k in range(8):
        own_ref[k, :CHUNK] = grads[pl.ds(pl.multiple_of(k * 2 * CHUNK + core * CHUNK, 8), CHUNK)]
        other_ref[k, :CHUNK] = grads[pl.ds(pl.multiple_of(k * 2 * CHUNK + (1 - core) * CHUNK, 8), CHUNK)]
        own_ref[k, CHUNK:] = counts
        other_ref[k, CHUNK:] = counts


def scale_kernel(step_ref, user_ref, v_ref, q_ref, o_ref):
    total = v_ref[0]
    for k in range(1, 8):
        total = total + v_ref[k]
    scales = step_ref[1] / (BLK * (1.0 + total[CHUNK : CHUNK + 1]))
    lane1 = lanes((1, BLK))
    for k in range(3):
        block = (user_ref[0] * 3 + k) // 4
        t = jnp.sum(jnp.where(lane1 == block, scales, 0.0), axis=1, keepdims=True)
        start = pl.multiple_of(user_ref[0] * CHUNK + k * 32, 8)
        o_ref[k * 32 : (k + 1) * 32] = q_ref[pl.ds(start, 32)] + t * total[k * 32 : (k + 1) * 32]


def spread_kernel(core_ref, own_ref, other_ref, o_ref):
    core = core_ref[0]
    for k in range(8):
        o_ref[k, pl.ds(pl.multiple_of(core * CHUNK, 8), CHUNK)] = own_ref[...]
        o_ref[k, pl.ds(pl.multiple_of((1 - core) * CHUNK, 8), CHUNK)] = other_ref[...]


def near(value):
    return pltpu.with_memory_space_constraint(value, pltpu.VMEM)


def far(value):
    return pltpu.with_memory_space_constraint(value, pltpu.HBM)


def call(kernel, out_shapes, specs, scratch=(), limit=8):
    single = len(out_shapes) == 1
    return pl.pallas_call(
        kernel,
        out_shape=out_shapes[0] if single else out_shapes,
        in_specs=specs,
        out_specs=VMEM if single else [VMEM] * len(out_shapes),
        scratch_shapes=scratch,
        compiler_params=pltpu.CompilerParams(vmem_limit_bytes=limit << 20),
    )


def body(ratings, presence, user_factors, item_factors, step_sizes):
    user = lax.axis_index("user")
    core = lax.rem(user, 2)
    user1, core1 = user.reshape(1), core.reshape(1)
    swap = [(k, k ^ 1) for k in range(16)]
    chips = [[k + 2 * j for j in range(8)] for k in range(2)]
    x = call(
        user_kernel,
        [pltpu.VMEM((PIECES, PIECE, BLK), F32)],
        [SMEM, HBM, HBM, HBM],
        [
            pltpu.VMEM((USERS, ITEMS), BF16),
            pltpu.VMEM((USERS, BLK), F32),
            pltpu.VMEM((ITEMS, BLK), F32),
            pltpu.VMEM((ITEMS, 2 * BLK), BF16),
            pltpu.VMEM((IB, BLK, BLK), F32),
            pltpu.VMEM((UB * 64, BLK), F32),
            pltpu.SemaphoreType.DMA((UB,)),
            pltpu.SemaphoreType.DMA((4,)),
            pltpu.SemaphoreType.DMA,
        ],
        limit=16,
    )(presence, far(ratings), far(user_factors), far(item_factors))
    y = lax.all_to_all(x, "item", 0, 0, tiled=True)
    z = call(total_kernel, [pltpu.VMEM((PIECES, PIECE, BLK), F32)], [VMEM])(near(y))
    z = lax.all_to_all(z, "item", 0, 0, tiled=True)
    new_users, own, other = call(
        item_kernel,
        [
            jax.ShapeDtypeStruct((USERS, BLK), F32),
            pltpu.VMEM((8, CHUNK + 8, BLK), F32),
            pltpu.VMEM((8, CHUNK + 8, BLK), F32),
        ],
        [SMEM, SMEM, SMEM, HBM, VMEM, VMEM, VMEM],
        [
            pltpu.VMEM((USERS, ITEMS), BF16),
            pltpu.VMEM((2 * BLK, USERS), BF16),
            pltpu.VMEM((UB, BLK, BLK), F32),
            pltpu.VMEM((ITEMS, BLK), F32),
            pltpu.SemaphoreType.DMA((UB,)),
        ],
        limit=16,
    )(presence, step_sizes, core1, far(ratings), near(user_factors), near(item_factors), near(z))
    v = own + lax.ppermute(other, "user", swap)
    v = lax.all_to_all(v, "user", 0, 0, tiled=True, axis_index_groups=chips)
    owned = call(scale_kernel, [pltpu.VMEM((CHUNK, BLK), F32)], [SMEM, SMEM, VMEM, VMEM])(
        step_sizes, user1, near(v), near(item_factors)
    )
    partner = lax.ppermute(owned, "user", swap)
    w = call(spread_kernel, [pltpu.VMEM((8, 2 * CHUNK, BLK), F32)], [SMEM, VMEM, VMEM])(
        core1, near(owned), near(partner)
    )
    w = lax.all_to_all(w, "user", 0, 0, tiled=True, axis_index_groups=chips)
    return new_users, w.reshape(ITEMS, BLK)


def solution(mesh):
    return jax.shard_map(
        body,
        mesh=mesh,
        in_specs=(P("user", "item"), P("user", "item"), P("user", None), P("item", None), P()),
        out_specs=(P("user", None), P("item", None)),
        check_vma=False,
    )
```

```python
import jax
import jax.numpy as jnp
from jax import lax
from jax.experimental import pallas as pl
from jax.experimental.pallas import tpu as pltpu
from jax.sharding import PartitionSpec as P

BLK = 128
UB = 6
IB = 12
USERS = UB * BLK
ITEMS = IB * BLK
PIECES = 16
ROWS = USERS // PIECES
HROWS = UB * 64 // PIECES
PIECE = ROWS + HROWS + 8
CHUNK = ITEMS // 16
F32 = jnp.float32
BF16 = jnp.bfloat16
VMEM = pl.BlockSpec(memory_space=pltpu.VMEM)
SMEM = pl.BlockSpec(memory_space=pltpu.SMEM)
HBM = pl.BlockSpec(memory_space=pltpu.HBM)


def split(value, axis):
    high = value.astype(BF16)
    low = (value - high.astype(F32)).astype(BF16)
    return jnp.concatenate([high, low], axis=axis)


def halves(value):
    return value[:, :BLK] + value[:, BLK:]


def gram(both, turned):
    square = jnp.dot(turned, both, preferred_element_type=F32)
    return halves(square[:BLK] + square[BLK:])


def thirds(value):
    high = value.astype(BF16)
    rest = value - high.astype(F32)
    middle = rest.astype(BF16)
    return high, middle, (rest - middle.astype(F32)).astype(BF16)


def exact(a, b):
    ah, am, al = thirds(a)
    bh, bm, bl = thirds(b)
    left = jnp.concatenate([ah, am, ah, al], axis=1)
    near_zero = jnp.zeros_like(bl)
    right = jnp.concatenate(
        [
            jnp.concatenate([bh, bh, bl, bh], axis=0),
            jnp.concatenate([bm, bm, near_zero, near_zero], axis=0),
        ],
        axis=1,
    )
    return halves(jnp.dot(left, right, preferred_element_type=F32))


def lanes(shape):
    return lax.broadcasted_iota(jnp.int32, shape, 1)


def sublanes(shape):
    return lax.broadcasted_iota(jnp.int32, shape, 0)


def block(index):
    return slice(index * BLK, (index + 1) * BLK)


def present(m_ref, b, j):
    return m_ref[b, j].astype(F32)


def fetch(source, target, sem, parts):
    rows = source.shape[0] // parts
    copies = []
    for k in range(parts):
        part = pl.ds(k * rows, rows)
        copies.append(pltpu.make_async_copy(source.at[part], target.at[part], sem.at[k]))
        copies[-1].start()
    return copies


def arrive(copies):
    for copy in copies:
        copy.wait()


def keep_present(m_ref, r_ref, b):
    for j in range(IB):
        r_ref[block(b), block(j)] = r_ref[block(b), block(j)] * present(m_ref, b, j).astype(BF16)


def user_kernel(m_ref, r_hbm, p_hbm, q_hbm, x_ref, r_ref, p_ref, q_ref, qcat, grams, packed, r_sem, q_sem, p_sem):
    q_copies = fetch(q_hbm, q_ref, q_sem, 4)
    p_copies = fetch(p_hbm, p_ref, p_sem, 2)
    r_copies = fetch(r_hbm, r_ref, r_sem, UB)
    arrive(q_copies)
    for j in range(IB):
        q = q_ref[block(j)]
        both = split(q, 1)
        qcat[block(j)] = both
        grams[j] = gram(both, split(q.T, 0))
    row64, lane64 = sublanes((64, BLK)), lanes((64, BLK))
    extra_row, extra_lane = sublanes((8, BLK)), lanes((8, BLK))
    extra = jnp.zeros((8, BLK), F32)
    arrive(p_copies + r_copies)
    for half in range(2):
        three = range(half * 3, half * 3 + 3)
        corrections = []
        for b in three:
            h = jnp.zeros((BLK, BLK), F32)
            count = jnp.int32(0)
            for j in range(IB):
                h = h + present(m_ref, b, j) * grams[j]
                count = count + m_ref[b, j]
            turned = jnp.concatenate([h[64:, 64:], h[64:, :64]], axis=1)
            packed[b * 64 : (b + 1) * 64] = jnp.where((lane64 < 64) & (lane64 > row64), turned, h[:64])
            diagonal = jnp.sum(jnp.where(lane64 == row64 + 64, h[64:], 0.0), axis=0, keepdims=True)
            extra = extra + jnp.where(extra_row == b, jnp.broadcast_to(diagonal, (8, BLK)), 0.0)
            extra = extra + jnp.where((extra_row == 6) & (extra_lane == b), count.astype(F32), 0.0)
            corrections.append(exact(p_ref[block(b)], h))
            keep_present(m_ref, r_ref, b)
        found = halves(
            jnp.dot(r_ref[half * 3 * BLK : (half + 1) * 3 * BLK], qcat[...], preferred_element_type=F32)
        )
        d = found - jnp.concatenate(corrections, axis=0)
        for k in range(8):
            x_ref[half * 8 + k, :ROWS] = d[k * ROWS : (k + 1) * ROWS]
    for piece in range(PIECES):
        x_ref[piece, ROWS : ROWS + HROWS] = packed[piece * HROWS : (piece + 1) * HROWS]
        x_ref[piece, ROWS + HROWS :] = extra if piece == 0 else jnp.zeros((8, BLK), F32)


def total_kernel(y_ref, z_ref):
    total = y_ref[0]
    for k in range(1, PIECES):
        total = total + y_ref[k]
    for k in range(PIECES):
        z_ref[k] = total


def item_kernel(
    m_ref, step_ref, r_hbm, p_ref, q_ref, z_ref, new_ref, own_ref, other_ref, r_ref, turned_ref, grams, grads, sem
):
    copies = fetch(r_hbm, r_ref, sem, UB)
    extra = z_ref[0, ROWS + HROWS :]
    scales = step_ref[0] / (BLK * (1.0 + extra[6:7]))
    row64, lane64 = sublanes((64, BLK)), lanes((64, BLK))
    for b in range(UB):
        tiles = []
        for k in range(0, BLK, 16):
            piece, at = divmod(b * BLK + k, ROWS)
            tiles.append(z_ref[piece, at : at + 16])
        d = jnp.concatenate(tiles, axis=0)
        tiles = []
        for k in range(0, 64, 8):
            piece, at = divmod(b * 64 + k, HROWS)
            tiles.append(z_ref[piece, ROWS + at : ROWS + at + 8])
        half = jnp.concatenate(tiles, axis=0)
        turned = jnp.concatenate([half[:, 64:], half[:, :64]], axis=1)
        top = jnp.where(lane64 < row64, half, jnp.where(lane64 == row64, 0.5 * half, 0.0))
        top = jnp.where(lane64 >= 64, half, top)
        bottom = jnp.where(lane64 > row64 + 64, turned, 0.0)
        bottom = jnp.where(lane64 == row64 + 64, 0.5 * extra[b : b + 1], bottom)
        w = jnp.concatenate([top, bottom], axis=0)
        s = scales[:, b : b + 1]
        new = p_ref[block(b)] + (2.0 * s) * d - (s * s) * exact(d, w + w.T)
        new_ref[block(b)] = new
        turned = split(new.T, 0)
        turned_ref[:, block(b)] = turned
        grams[b] = gram(split(new, 1), turned)
    arrive(copies)
    for b in range(UB):
        keep_present(m_ref, r_ref, b)
    counts = jnp.zeros((8, BLK), F32)
    lane8 = lanes((8, BLK))
    for pair in range(IB // 2):
        found = jnp.dot(
            turned_ref[...], r_ref[:, pair * 2 * BLK : (pair + 1) * 2 * BLK], preferred_element_type=F32
        )
        found = found[:BLK] + found[BLK:]
        for k in range(2):
            j = pair * 2 + k
            s = jnp.zeros((BLK, BLK), F32)
            count = jnp.int32(0)
            for b in range(UB):
                s = s + present(m_ref, b, j) * grams[b]
                count = count + m_ref[b, j]
            counts = counts + jnp.where(lane8 == j, count.astype(F32), 0.0)
            grads[block(j)] = found[:, block(k)].T - exact(q_ref[block(j)], s)
    core = lax.rem(lax.axis_index("user"), 2)
    for k in range(8):
        own_ref[k, :CHUNK] = grads[pl.ds(pl.multiple_of(k * 2 * CHUNK + core * CHUNK, 8), CHUNK)]
        other_ref[k, :CHUNK] = grads[pl.ds(pl.multiple_of(k * 2 * CHUNK + (1 - core) * CHUNK, 8), CHUNK)]
        own_ref[k, CHUNK:] = counts
        other_ref[k, CHUNK:] = counts


def scale_kernel(step_ref, v_ref, q_ref, o_ref):
    user = lax.axis_index("user")
    total = v_ref[0]
    for k in range(1, 8):
        total = total + v_ref[k]
    scales = step_ref[1] / (BLK * (1.0 + total[CHUNK : CHUNK + 1]))
    lane1 = lanes((1, BLK))
    for k in range(3):
        block = (user * 3 + k) // 4
        t = jnp.sum(jnp.where(lane1 == block, scales, 0.0), axis=1, keepdims=True)
        start = pl.multiple_of(user * CHUNK + k * 32, 8)
        new = q_ref[pl.ds(start, 32)] + t * total[k * 32 : (k + 1) * 32]
        for piece in range(8):
            o_ref[piece, k * 32 : (k + 1) * 32] = new


def join_kernel(own_ref, other_ref, o_hbm, sem):
    core = lax.rem(lax.axis_index("user"), 2)
    copies = []
    for k in range(8):
        for n, (ref, place) in enumerate(((own_ref, core), (other_ref, 1 - core))):
            rows = pl.ds(pl.multiple_of(k * 2 * CHUNK + place * CHUNK, 8), CHUNK)
            copies.append(pltpu.make_async_copy(ref.at[k], o_hbm.at[rows], sem.at[k * 2 + n]))
            copies[-1].start()
    arrive(copies)


def near(value):
    return pltpu.with_memory_space_constraint(value, pltpu.VMEM)


def far(value):
    return pltpu.with_memory_space_constraint(value, pltpu.HBM)


def call(kernel, out_shapes, specs, scratch=(), limit=8, out_specs=VMEM):
    single = len(out_shapes) == 1
    return pl.pallas_call(
        kernel,
        out_shape=out_shapes[0] if single else out_shapes,
        in_specs=specs,
        out_specs=out_specs if single else [out_specs] * len(out_shapes),
        scratch_shapes=scratch,
        compiler_params=pltpu.CompilerParams(vmem_limit_bytes=limit << 20),
    )


def body(ratings, presence, user_factors, item_factors, step_sizes):
    swap = [(k, k ^ 1) for k in range(16)]
    chips = [[k + 2 * j for j in range(8)] for k in range(2)]
    x = call(
        user_kernel,
        [pltpu.VMEM((PIECES, PIECE, BLK), F32)],
        [SMEM, HBM, HBM, HBM],
        [
            pltpu.VMEM((USERS, ITEMS), BF16),
            pltpu.VMEM((USERS, BLK), F32),
            pltpu.VMEM((ITEMS, BLK), F32),
            pltpu.VMEM((ITEMS, 2 * BLK), BF16),
            pltpu.VMEM((IB, BLK, BLK), F32),
            pltpu.VMEM((UB * 64, BLK), F32),
            pltpu.SemaphoreType.DMA((UB,)),
            pltpu.SemaphoreType.DMA((4,)),
            pltpu.SemaphoreType.DMA((2,)),
        ],
        limit=16,
    )(presence, far(ratings), far(user_factors), far(item_factors))
    y = lax.all_to_all(x, "item", 0, 0, tiled=True)
    z = call(total_kernel, [pltpu.VMEM((PIECES, PIECE, BLK), F32)], [VMEM])(near(y))
    z = lax.all_to_all(z, "item", 0, 0, tiled=True)
    new_users, own, other = call(
        item_kernel,
        [
            jax.ShapeDtypeStruct((USERS, BLK), F32),
            pltpu.VMEM((8, CHUNK + 8, BLK), F32),
            pltpu.VMEM((8, CHUNK + 8, BLK), F32),
        ],
        [SMEM, SMEM, HBM, VMEM, VMEM, VMEM],
        [
            pltpu.VMEM((USERS, ITEMS), BF16),
            pltpu.VMEM((2 * BLK, USERS), BF16),
            pltpu.VMEM((UB, BLK, BLK), F32),
            pltpu.VMEM((ITEMS, BLK), F32),
            pltpu.SemaphoreType.DMA((UB,)),
        ],
        limit=16,
    )(presence, step_sizes, far(ratings), near(user_factors), near(item_factors), near(z))
    v = own + lax.ppermute(other, "user", swap)
    v = lax.all_to_all(v, "user", 0, 0, tiled=True, axis_index_groups=chips)
    owned = call(scale_kernel, [pltpu.VMEM((8, CHUNK, BLK), F32)], [SMEM, VMEM, VMEM])(
        step_sizes, near(v), near(item_factors)
    )
    mine = lax.all_to_all(owned, "user", 0, 0, tiled=True, axis_index_groups=chips)
    theirs = lax.ppermute(mine, "user", swap)
    new_items = call(
        join_kernel,
        [pltpu.HBM((ITEMS, BLK), F32)],
        [VMEM, VMEM],
        [pltpu.SemaphoreType.DMA((16,))],
        out_specs=HBM,
    )(near(mine), near(theirs))
    return new_users, new_items


def solution(mesh):
    return jax.shard_map(
        body,
        mesh=mesh,
        in_specs=(P("user", "item"), P("user", "item"), P("user", None), P("item", None), P()),
        out_specs=(P("user", None), P("item", None)),
        check_vma=False,
    )
```

```python
import jax
import jax.numpy as jnp
from jax import lax
from jax.experimental import pallas as pl
from jax.experimental.pallas import tpu as pltpu
from jax.sharding import PartitionSpec as P

BLK = 128
UB = 6
IB = 12
USERS = UB * BLK
ITEMS = IB * BLK
PIECES = 16
ROWS = USERS // PIECES
HROWS = UB * 64 // PIECES
SENT = ROWS + HROWS
PIECE = SENT + 8
CHUNK = ITEMS // 16
F32 = jnp.float32
BF16 = jnp.bfloat16
VMEM = pl.BlockSpec(memory_space=pltpu.VMEM)
SMEM = pl.BlockSpec(memory_space=pltpu.SMEM)
HBM = pl.BlockSpec(memory_space=pltpu.HBM)


def split(value, axis):
    high = value.astype(BF16)
    low = (value - high.astype(F32)).astype(BF16)
    return jnp.concatenate([high, low], axis=axis)


def halves(value):
    return value[:, :BLK] + value[:, BLK:]


def gram(both, turned):
    square = jnp.dot(turned, both, preferred_element_type=F32)
    return halves(square[:BLK] + square[BLK:])


def thirds(value):
    high = value.astype(BF16)
    rest = value - high.astype(F32)
    middle = rest.astype(BF16)
    return high, middle, (rest - middle.astype(F32)).astype(BF16)


def exact(a, b):
    ah, am, al = thirds(a)
    bh, bm, bl = thirds(b)
    left = jnp.concatenate([ah, am, ah, al], axis=1)
    near_zero = jnp.zeros_like(bl)
    right = jnp.concatenate(
        [
            jnp.concatenate([bh, bh, bl, bh], axis=0),
            jnp.concatenate([bm, bm, near_zero, near_zero], axis=0),
        ],
        axis=1,
    )
    return halves(jnp.dot(left, right, preferred_element_type=F32))


def lanes(shape):
    return lax.broadcasted_iota(jnp.int32, shape, 1)


def sublanes(shape):
    return lax.broadcasted_iota(jnp.int32, shape, 0)


def block(index):
    return slice(index * BLK, (index + 1) * BLK)


def present(m_ref, b, j):
    return m_ref[b, j].astype(F32)


def fetch(source, target, sem, parts):
    rows = source.shape[0] // parts
    copies = []
    for k in range(parts):
        part = pl.ds(k * rows, rows)
        copies.append(pltpu.make_async_copy(source.at[part], target.at[part], sem.at[k]))
        copies[-1].start()
    return copies


def arrive(copies):
    for copy in copies:
        copy.wait()


def keep_present(m_ref, r_ref, kept, b):
    for j in range(IB):
        kept[block(b), block(j)] = r_ref[block(b), block(j)] * present(m_ref, b, j).astype(BF16)


def user_kernel(
    m_hbm, r_hbm, p_hbm, q_hbm, x_ref, m_ref, r_ref, p_ref, q_ref, qcat, grams, packed, r_sem, q_sem, p_sem, m_sem
):
    m_copy = pltpu.make_async_copy(m_hbm, m_ref, m_sem)
    m_copy.start()
    q_copies = fetch(q_hbm, q_ref, q_sem, 4)
    p_copies = fetch(p_hbm, p_ref, p_sem, 2)
    r_copies = fetch(r_hbm, r_ref, r_sem, UB)
    arrive(q_copies)
    for j in range(IB):
        q = q_ref[block(j)]
        both = split(q, 1)
        qcat[block(j)] = both
        grams[j] = gram(both, split(q.T, 0))
    row64, lane64 = sublanes((64, BLK)), lanes((64, BLK))
    extra_row, extra_lane = sublanes((8, BLK)), lanes((8, BLK))
    extra = jnp.zeros((8, BLK), F32)
    arrive([m_copy] + p_copies + r_copies)
    for half in range(2):
        three = range(half * 3, half * 3 + 3)
        corrections = []
        for b in three:
            h = jnp.zeros((BLK, BLK), F32)
            count = jnp.int32(0)
            for j in range(IB):
                h = h + present(m_ref, b, j) * grams[j]
                count = count + m_ref[b, j]
            turned = jnp.concatenate([h[64:, 64:], h[64:, :64]], axis=1)
            packed[b * 64 : (b + 1) * 64] = jnp.where((lane64 < 64) & (lane64 > row64), turned, h[:64])
            diagonal = jnp.sum(jnp.where(lane64 == row64 + 64, h[64:], 0.0), axis=0, keepdims=True)
            extra = extra + jnp.where(extra_row == b, jnp.broadcast_to(diagonal, (8, BLK)), 0.0)
            extra = extra + jnp.where((extra_row == 6) & (extra_lane == b), count.astype(F32), 0.0)
            corrections.append(exact(p_ref[block(b)], h))
            keep_present(m_ref, r_ref, r_ref, b)
        found = halves(
            jnp.dot(r_ref[half * 3 * BLK : (half + 1) * 3 * BLK], qcat[...], preferred_element_type=F32)
        )
        d = found - jnp.concatenate(corrections, axis=0)
        for k in range(8):
            x_ref[half * 8 + k, :ROWS] = d[k * ROWS : (k + 1) * ROWS]
    for piece in range(PIECES):
        x_ref[piece, ROWS : ROWS + HROWS] = packed[piece * HROWS : (piece + 1) * HROWS]
        x_ref[piece, SENT:] = extra


def total_kernel(y_ref, z_ref, extra_ref):
    total = y_ref[0]
    for k in range(1, PIECES):
        total = total + y_ref[k]
    extra_ref[...] = total[SENT:]
    for k in range(PIECES):
        z_ref[k] = total[:SENT]


def item_kernel(
    m_ref, step_ref, r_ref, p_ref, q_ref, z_ref, extra_ref, new_ref, own_ref, other_ref, kept, turned_ref, grams, grads
):
    extra = extra_ref[...]
    scales = step_ref[0] / (BLK * (1.0 + extra[6:7]))
    row64, lane64 = sublanes((64, BLK)), lanes((64, BLK))
    for b in range(UB):
        tiles = []
        for k in range(0, BLK, 16):
            piece, at = divmod(b * BLK + k, ROWS)
            tiles.append(z_ref[piece, at : at + 16])
        d = jnp.concatenate(tiles, axis=0)
        tiles = []
        for k in range(0, 64, 8):
            piece, at = divmod(b * 64 + k, HROWS)
            tiles.append(z_ref[piece, ROWS + at : ROWS + at + 8])
        half = jnp.concatenate(tiles, axis=0)
        turned = jnp.concatenate([half[:, 64:], half[:, :64]], axis=1)
        top = jnp.where(lane64 < row64, half, jnp.where(lane64 == row64, 0.5 * half, 0.0))
        top = jnp.where(lane64 >= 64, half, top)
        bottom = jnp.where(lane64 > row64 + 64, turned, 0.0)
        bottom = jnp.where(lane64 == row64 + 64, 0.5 * extra[b : b + 1], bottom)
        w = jnp.concatenate([top, bottom], axis=0)
        s = scales[:, b : b + 1]
        new = p_ref[block(b)] + (2.0 * s) * d - (s * s) * exact(d, w + w.T)
        new_ref[block(b)] = new
        turned = split(new.T, 0)
        turned_ref[:, block(b)] = turned
        grams[b] = gram(split(new, 1), turned)
        keep_present(m_ref, r_ref, kept, b)
    counts = jnp.zeros((8, BLK), F32)
    lane8 = lanes((8, BLK))
    for pair in range(IB // 2):
        found = jnp.dot(
            turned_ref[...], kept[:, pair * 2 * BLK : (pair + 1) * 2 * BLK], preferred_element_type=F32
        )
        found = found[:BLK] + found[BLK:]
        for k in range(2):
            j = pair * 2 + k
            s = jnp.zeros((BLK, BLK), F32)
            count = jnp.int32(0)
            for b in range(UB):
                s = s + present(m_ref, b, j) * grams[b]
                count = count + m_ref[b, j]
            counts = counts + jnp.where(lane8 == j, count.astype(F32), 0.0)
            grads[block(j)] = found[:, block(k)].T - exact(q_ref[block(j)], s)
    user = lax.axis_index("user")
    core = lax.rem(user, 2)
    step = jnp.where(user == 0, step_ref[1], 0.0)
    counts = jnp.where(sublanes((8, BLK)) == 0, counts, step)
    for k in range(8):
        own_ref[k, :CHUNK] = grads[pl.ds(pl.multiple_of(k * 2 * CHUNK + core * CHUNK, 8), CHUNK)]
        other_ref[k, :CHUNK] = grads[pl.ds(pl.multiple_of(k * 2 * CHUNK + (1 - core) * CHUNK, 8), CHUNK)]
        own_ref[k, CHUNK:] = counts
        other_ref[k, CHUNK:] = counts


def scale_kernel(v_ref, q_ref, o_ref):
    user = lax.axis_index("user")
    total = v_ref[0]
    for k in range(1, 8):
        total = total + v_ref[k]
    scales = total[CHUNK + 1 : CHUNK + 2] / (BLK * (1.0 + total[CHUNK : CHUNK + 1]))
    lane1 = lanes((1, BLK))
    for k in range(3):
        block = (user * 3 + k) // 4
        t = jnp.sum(jnp.where(lane1 == block, scales, 0.0), axis=1, keepdims=True)
        start = pl.multiple_of(user * CHUNK + k * 32, 8)
        new = q_ref[pl.ds(start, 32)] + t * total[k * 32 : (k + 1) * 32]
        for piece in range(8):
            o_ref[piece, k * 32 : (k + 1) * 32] = new


def join_kernel(own_ref, other_ref, o_hbm, sem):
    core = lax.rem(lax.axis_index("user"), 2)
    copies = []
    for k in range(8):
        for n, (ref, place) in enumerate(((own_ref, core), (other_ref, 1 - core))):
            rows = pl.ds(pl.multiple_of(k * 2 * CHUNK + place * CHUNK, 8), CHUNK)
            copies.append(pltpu.make_async_copy(ref.at[k], o_hbm.at[rows], sem.at[k * 2 + n]))
            copies[-1].start()
    arrive(copies)


def near(value):
    return pltpu.with_memory_space_constraint(value, pltpu.VMEM)


def far(value):
    return pltpu.with_memory_space_constraint(value, pltpu.HBM)


def call(kernel, out_shapes, specs, scratch=(), limit=8, out_specs=VMEM):
    single = len(out_shapes) == 1
    return pl.pallas_call(
        kernel,
        out_shape=out_shapes[0] if single else out_shapes,
        in_specs=specs,
        out_specs=out_specs if single else [out_specs] * len(out_shapes),
        scratch_shapes=scratch,
        compiler_params=pltpu.CompilerParams(vmem_limit_bytes=limit << 20),
    )


def body(ratings, presence, user_factors, item_factors, step_sizes):
    swap = [(k, k ^ 1) for k in range(16)]
    chips = [[k + 2 * j for j in range(8)] for k in range(2)]
    x = call(
        user_kernel,
        [pltpu.VMEM((PIECES, PIECE, BLK), F32)],
        [HBM, HBM, HBM, HBM],
        [
            pltpu.SMEM((UB, IB), jnp.int32),
            pltpu.VMEM((USERS, ITEMS), BF16),
            pltpu.VMEM((USERS, BLK), F32),
            pltpu.VMEM((ITEMS, BLK), F32),
            pltpu.VMEM((ITEMS, 2 * BLK), BF16),
            pltpu.VMEM((IB, BLK, BLK), F32),
            pltpu.VMEM((UB * 64, BLK), F32),
            pltpu.SemaphoreType.DMA((UB,)),
            pltpu.SemaphoreType.DMA((4,)),
            pltpu.SemaphoreType.DMA((2,)),
            pltpu.SemaphoreType.DMA,
        ],
        limit=16,
    )(far(presence), far(ratings), far(user_factors), far(item_factors))
    y = lax.all_to_all(x, "item", 0, 0, tiled=True)
    z, extra = call(
        total_kernel, [pltpu.VMEM((PIECES, SENT, BLK), F32), pltpu.VMEM((8, BLK), F32)], [VMEM]
    )(near(y))
    z = lax.all_to_all(z, "item", 0, 0, tiled=True)
    new_users, own, other = call(
        item_kernel,
        [
            jax.ShapeDtypeStruct((USERS, BLK), F32),
            pltpu.VMEM((8, CHUNK + 8, BLK), F32),
            pltpu.VMEM((8, CHUNK + 8, BLK), F32),
        ],
        [SMEM, SMEM, VMEM, VMEM, VMEM, VMEM, VMEM],
        [
            pltpu.VMEM((USERS, ITEMS), BF16),
            pltpu.VMEM((2 * BLK, USERS), BF16),
            pltpu.VMEM((UB, BLK, BLK), F32),
            pltpu.VMEM((ITEMS, BLK), F32),
        ],
        limit=16,
    )(presence, step_sizes, near(ratings), near(user_factors), near(item_factors), near(z), near(extra))
    v = own + lax.ppermute(other, "user", swap)
    v = lax.all_to_all(v, "user", 0, 0, tiled=True, axis_index_groups=chips)
    owned = call(scale_kernel, [pltpu.VMEM((8, CHUNK, BLK), F32)], [VMEM, VMEM])(
        near(v), near(item_factors)
    )
    mine = lax.all_to_all(owned, "user", 0, 0, tiled=True, axis_index_groups=chips)
    theirs = lax.ppermute(mine, "user", swap)
    new_items = call(
        join_kernel,
        [pltpu.HBM((ITEMS, BLK), F32)],
        [VMEM, VMEM],
        [pltpu.SemaphoreType.DMA((16,))],
        out_specs=HBM,
    )(near(mine), near(theirs))
    return new_users, new_items


def solution(mesh):
    return jax.shard_map(
        body,
        mesh=mesh,
        in_specs=(P("user", "item"), P("user", "item"), P("user", None), P("item", None), P()),
        out_specs=(P("user", None), P("item", None)),
        check_vma=False,
    )
```

```python
import jax
import jax.numpy as jnp
from jax import lax
from jax.experimental import pallas as pl
from jax.experimental.pallas import tpu as pltpu
from jax.sharding import PartitionSpec as P

BLK = 128
UB = 6
IB = 12
USERS = UB * BLK
ITEMS = IB * BLK
PIECES = 16
ROWS = USERS // PIECES
HROWS = UB * 64 // PIECES
SENT = ROWS + HROWS
PIECE = SENT + 8
CHUNK = ITEMS // 16
F32 = jnp.float32
BF16 = jnp.bfloat16
VMEM = pl.BlockSpec(memory_space=pltpu.VMEM)
SMEM = pl.BlockSpec(memory_space=pltpu.SMEM)
HBM = pl.BlockSpec(memory_space=pltpu.HBM)


def split(value, axis):
    high = value.astype(BF16)
    low = (value - high.astype(F32)).astype(BF16)
    return jnp.concatenate([high, low], axis=axis)


def halves(value):
    return value[:, :BLK] + value[:, BLK:]


def gram(both, turned):
    square = jnp.dot(turned, both, preferred_element_type=F32)
    return halves(square[:BLK] + square[BLK:])


def thirds(value):
    high = value.astype(BF16)
    rest = value - high.astype(F32)
    middle = rest.astype(BF16)
    return high, middle, (rest - middle.astype(F32)).astype(BF16)


def exact(a, b):
    ah, am, al = thirds(a)
    bh, bm, bl = thirds(b)
    left = jnp.concatenate([ah, am, ah, al], axis=1)
    near_zero = jnp.zeros_like(bl)
    right = jnp.concatenate(
        [
            jnp.concatenate([bh, bh, bl, bh], axis=0),
            jnp.concatenate([bm, bm, near_zero, near_zero], axis=0),
        ],
        axis=1,
    )
    return halves(jnp.dot(left, right, preferred_element_type=F32))


def lanes(shape):
    return lax.broadcasted_iota(jnp.int32, shape, 1)


def sublanes(shape):
    return lax.broadcasted_iota(jnp.int32, shape, 0)


def block(index):
    return slice(index * BLK, (index + 1) * BLK)


def present(m_ref, b, j):
    return m_ref[b, j].astype(F32)


def fetch(source, target, sem, parts):
    rows = source.shape[0] // parts
    copies = []
    for k in range(parts):
        part = pl.ds(k * rows, rows)
        copies.append(pltpu.make_async_copy(source.at[part], target.at[part], sem.at[k]))
        copies[-1].start()
    return copies


def arrive(copies):
    for copy in copies:
        copy.wait()


def only_present(m_ref, r_ref, blocks, columns, first, count):
    return jnp.concatenate(
        [
            jnp.concatenate(
                [
                    r_ref[block(b), pl.ds(pl.multiple_of(columns + k * BLK, BLK), BLK)]
                    * present(m_ref, b, first + k).astype(BF16)
                    for k in range(count)
                ],
                axis=1,
            )
            for b in blocks
        ],
        axis=0,
    )


def user_kernel(
    m_hbm, r_hbm, p_hbm, q_hbm, x_ref, m_ref, r_ref, p_ref, q_ref, qcat, grams, packed, r_sem, q_sem, p_sem, m_sem
):
    m_copy = pltpu.make_async_copy(m_hbm, m_ref, m_sem)
    m_copy.start()
    q_copies = fetch(q_hbm, q_ref, q_sem, 4)
    p_copies = fetch(p_hbm, p_ref, p_sem, 2)
    r_copies = fetch(r_hbm, r_ref, r_sem, UB)
    arrive(q_copies)
    for j in range(IB):
        q = q_ref[block(j)]
        both = split(q, 1)
        qcat[block(j)] = both
        grams[j] = gram(both, split(q.T, 0))
    row64, lane64 = sublanes((64, BLK)), lanes((64, BLK))
    extra_row, extra_lane = sublanes((8, BLK)), lanes((8, BLK))
    extra = jnp.zeros((8, BLK), F32)
    arrive([m_copy] + p_copies + r_copies)
    for half in range(2):
        three = range(half * 3, half * 3 + 3)
        corrections = []
        for b in three:
            h = jnp.zeros((BLK, BLK), F32)
            count = jnp.int32(0)
            for j in range(IB):
                h = h + present(m_ref, b, j) * grams[j]
                count = count + m_ref[b, j]
            turned = jnp.concatenate([h[64:, 64:], h[64:, :64]], axis=1)
            packed[b * 64 : (b + 1) * 64] = jnp.where((lane64 < 64) & (lane64 > row64), turned, h[:64])
            diagonal = jnp.sum(jnp.where(lane64 == row64 + 64, h[64:], 0.0), axis=0, keepdims=True)
            extra = extra + jnp.where(extra_row == b, jnp.broadcast_to(diagonal, (8, BLK)), 0.0)
            extra = extra + jnp.where((extra_row == 6) & (extra_lane == b), count.astype(F32), 0.0)
            corrections.append(exact(p_ref[block(b)], h))
        masked = only_present(m_ref, r_ref, three, 0, 0, IB)
        found = halves(jnp.dot(masked, qcat[...], preferred_element_type=F32))
        d = found - jnp.concatenate(corrections, axis=0)
        for k in range(8):
            x_ref[half * 8 + k, :ROWS] = d[k * ROWS : (k + 1) * ROWS]
    for piece in range(PIECES):
        x_ref[piece, ROWS : ROWS + HROWS] = packed[piece * HROWS : (piece + 1) * HROWS]
        x_ref[piece, SENT:] = extra


def total_kernel(y_ref, z_ref, extra_ref):
    total = y_ref[0]
    for k in range(1, PIECES):
        total = total + y_ref[k]
    extra_ref[...] = total[SENT:]
    for k in range(PIECES):
        z_ref[k] = total[:SENT]


def item_kernel(
    m_ref, step_ref, r_ref, p_ref, q_ref, z_ref, extra_ref, new_ref, other_ref, turned_ref, grams
):
    extra = extra_ref[...]
    scales = step_ref[0] / (BLK * (1.0 + extra[6:7]))
    row64, lane64 = sublanes((64, BLK)), lanes((64, BLK))
    for b in range(UB):
        tiles = []
        for k in range(0, BLK, 16):
            piece, at = divmod(b * BLK + k, ROWS)
            tiles.append(z_ref[piece, at : at + 16])
        d = jnp.concatenate(tiles, axis=0)
        tiles = []
        for k in range(0, 64, 8):
            piece, at = divmod(b * 64 + k, HROWS)
            tiles.append(z_ref[piece, ROWS + at : ROWS + at + 8])
        half = jnp.concatenate(tiles, axis=0)
        turned = jnp.concatenate([half[:, 64:], half[:, :64]], axis=1)
        top = jnp.where(lane64 < row64, half, jnp.where(lane64 == row64, 0.5 * half, 0.0))
        top = jnp.where(lane64 >= 64, half, top)
        bottom = jnp.where(lane64 > row64 + 64, turned, 0.0)
        bottom = jnp.where(lane64 == row64 + 64, 0.5 * extra[b : b + 1], bottom)
        w = jnp.concatenate([top, bottom], axis=0)
        s = scales[:, b : b + 1]
        new = p_ref[block(b)] + (2.0 * s) * d - (s * s) * exact(d, w + w.T)
        new_ref[block(b)] = new
        turned = split(new.T, 0)
        turned_ref[:, block(b)] = turned
        grams[b] = gram(split(new, 1), turned)
    core = lax.rem(lax.axis_index("user"), 2)
    item_half(1 - core, m_ref, step_ref, r_ref, q_ref, turned_ref, grams, other_ref)


def item_half(side, m_ref, step_ref, r_ref, q_ref, turned_ref, grams, o_ref):
    counts = jnp.zeros((8, BLK), F32)
    row8, lane8 = sublanes((8, BLK)), lanes((8, BLK))
    for j in range(IB):
        count = jnp.int32(0)
        for b in range(UB):
            count = count + m_ref[b, j]
        counts = counts + jnp.where(lane8 == j, count.astype(F32), 0.0)
    step = jnp.where(lax.axis_index("user") == 0, step_ref[1], 0.0)
    counts = jnp.where(row8 == 0, counts, step)
    first = side * (IB // 2)
    for pair in range(IB // 4):
        columns = pl.multiple_of(side * (ITEMS // 2) + pair * 2 * BLK, BLK)
        masked = only_present(m_ref, r_ref, range(UB), columns, first + pair * 2, 2)
        found = jnp.dot(turned_ref[...], masked, preferred_element_type=F32)
        found = found[:BLK] + found[BLK:]
        for k in range(2):
            s = jnp.zeros((BLK, BLK), F32)
            for b in range(UB):
                s = s + present(m_ref, b, first + pair * 2 + k) * grams[b]
            q = q_ref[pl.ds(pl.multiple_of(columns + k * BLK, BLK), BLK)]
            grad = found[:, block(k)].T - exact(q, s)
            for part in range(4):
                piece, at = divmod((pair * 2 + k) * 4 + part, 3)
                o_ref[piece, at * 32 : (at + 1) * 32] = grad[part * 32 : (part + 1) * 32]
    for piece in range(8):
        o_ref[piece, CHUNK:] = counts


def own_kernel(m_ref, step_ref, r_ref, q_ref, turned_ref, grams, own_ref):
    core = lax.rem(lax.axis_index("user"), 2)
    item_half(core, m_ref, step_ref, r_ref, q_ref, turned_ref, grams, own_ref)


def scale_kernel(v_ref, q_ref, o_ref):
    user = lax.axis_index("user")
    total = v_ref[0]
    for k in range(1, 8):
        total = total + v_ref[k]
    scales = total[CHUNK + 1 : CHUNK + 2] / (BLK * (1.0 + total[CHUNK : CHUNK + 1]))
    lane1 = lanes((1, BLK))
    for k in range(3):
        place = lax.rem(user, 2) * 24 + (user // 2) * 3 + k
        t = jnp.sum(jnp.where(lane1 == place // 4, scales, 0.0), axis=1, keepdims=True)
        start = pl.multiple_of(place * 32, 8)
        new = q_ref[pl.ds(start, 32)] + t * total[k * 32 : (k + 1) * 32]
        for piece in range(8):
            o_ref[piece, k * 32 : (k + 1) * 32] = new


def place_kernel(flip, half_ref, whole, o_hbm, sem):
    core = lax.rem(lax.axis_index("user"), 2)
    side = 1 - core if flip else core
    copies = []
    for k in range(8):
        rows = pl.ds(pl.multiple_of(side * (ITEMS // 2) + k * CHUNK, 8), CHUNK)
        copies.append(pltpu.make_async_copy(half_ref.at[k], o_hbm.at[rows], sem.at[k]))
        copies[-1].start()
    arrive(copies)


def place_own_kernel(half_ref, o_hbm, sem):
    place_kernel(False, half_ref, None, o_hbm, sem)


def place_other_kernel(half_ref, whole, o_hbm, sem):
    place_kernel(True, half_ref, whole, o_hbm, sem)


def near(value):
    return pltpu.with_memory_space_constraint(value, pltpu.VMEM)


def far(value):
    return pltpu.with_memory_space_constraint(value, pltpu.HBM)


def call(kernel, out_shapes, specs, scratch=(), limit=8, out_specs=VMEM, cost=None, alias={}):
    single = len(out_shapes) == 1
    return pl.pallas_call(
        kernel,
        out_shape=out_shapes[0] if single else out_shapes,
        in_specs=specs,
        out_specs=out_specs if single else [out_specs] * len(out_shapes),
        scratch_shapes=scratch,
        compiler_params=pltpu.CompilerParams(vmem_limit_bytes=limit << 20),
        cost_estimate=cost,
        input_output_aliases=alias,
    )


def body(ratings, presence, user_factors, item_factors, step_sizes):
    swap = [(k, k ^ 1) for k in range(16)]
    chips = [[k + 2 * j for j in range(8)] for k in range(2)]
    x = call(
        user_kernel,
        [pltpu.VMEM((PIECES, PIECE, BLK), F32)],
        [HBM, HBM, HBM, HBM],
        [
            pltpu.SMEM((UB, IB), jnp.int32),
            pltpu.VMEM((USERS, ITEMS), BF16),
            pltpu.VMEM((USERS, BLK), F32),
            pltpu.VMEM((ITEMS, BLK), F32),
            pltpu.VMEM((ITEMS, 2 * BLK), BF16),
            pltpu.VMEM((IB, BLK, BLK), F32),
            pltpu.VMEM((UB * 64, BLK), F32),
            pltpu.SemaphoreType.DMA((UB,)),
            pltpu.SemaphoreType.DMA((4,)),
            pltpu.SemaphoreType.DMA((2,)),
            pltpu.SemaphoreType.DMA,
        ],
        limit=16,
    )(far(presence), far(ratings), far(user_factors), far(item_factors))
    y = lax.all_to_all(x, "item", 0, 0, tiled=True)
    z, extra = call(
        total_kernel, [pltpu.VMEM((PIECES, SENT, BLK), F32), pltpu.VMEM((8, BLK), F32)], [VMEM]
    )(near(y))
    z = lax.all_to_all(z, "item", 0, 0, tiled=True)
    new_users, other, turned, grams = call(
        item_kernel,
        [
            jax.ShapeDtypeStruct((USERS, BLK), F32),
            pltpu.VMEM((8, CHUNK + 8, BLK), F32),
            pltpu.VMEM((2 * BLK, USERS), BF16),
            pltpu.VMEM((UB, BLK, BLK), F32),
        ],
        [SMEM, SMEM, VMEM, VMEM, VMEM, VMEM, VMEM],
        limit=16,
    )(presence, step_sizes, near(ratings), near(user_factors), near(item_factors), near(z), near(extra))
    received = lax.ppermute(other, "user", swap)
    own = call(
        own_kernel,
        [pltpu.VMEM((8, CHUNK + 8, BLK), F32)],
        [SMEM, SMEM, VMEM, VMEM, VMEM, VMEM],
        limit=16,
        cost=pl.CostEstimate(flops=1 << 32, bytes_accessed=1 << 23, transcendentals=0),
    )(presence, step_sizes, near(ratings), near(item_factors), near(turned), near(grams))
    v = own + received
    v = lax.all_to_all(v, "user", 0, 0, tiled=True, axis_index_groups=chips)
    owned = call(scale_kernel, [pltpu.VMEM((8, CHUNK, BLK), F32)], [VMEM, VMEM])(
        near(v), near(item_factors)
    )
    mine = lax.all_to_all(owned, "user", 0, 0, tiled=True, axis_index_groups=chips)
    theirs = lax.ppermute(mine, "user", swap)
    half = call(
        place_own_kernel,
        [pltpu.HBM((ITEMS, BLK), F32)],
        [VMEM],
        [pltpu.SemaphoreType.DMA((8,))],
        out_specs=HBM,
        cost=pl.CostEstimate(flops=1 << 30, bytes_accessed=1 << 22, transcendentals=0),
    )(near(mine))
    new_items = call(
        place_other_kernel,
        [pltpu.HBM((ITEMS, BLK), F32)],
        [VMEM, HBM],
        [pltpu.SemaphoreType.DMA((8,))],
        out_specs=HBM,
        alias={1: 0},
    )(near(theirs), half)
    return new_users, new_items


def solution(mesh):
    return jax.shard_map(
        body,
        mesh=mesh,
        in_specs=(P("user", "item"), P("user", "item"), P("user", None), P("item", None), P()),
        out_specs=(P("user", None), P("item", None)),
        check_vma=False,
    )
```

```python
import jax
import jax.numpy as jnp
from jax import lax
from jax.experimental import pallas as pl
from jax.experimental.pallas import tpu as pltpu
from jax.sharding import PartitionSpec as P

BLK = 128
UB = 6
IB = 12
USERS = UB * BLK
ITEMS = IB * BLK
PIECES = 16
ROWS = USERS // PIECES
HROWS = UB * 64 // PIECES
SENT = ROWS + HROWS
TILES = SENT // 4 + 1
CHUNK = ITEMS // 16
F32 = jnp.float32
BF16 = jnp.bfloat16
VMEM = pl.BlockSpec(memory_space=pltpu.VMEM)
SMEM = pl.BlockSpec(memory_space=pltpu.SMEM)
HBM = pl.BlockSpec(memory_space=pltpu.HBM)


def split(value, axis):
    high = value.astype(BF16)
    low = (value - high.astype(F32)).astype(BF16)
    return jnp.concatenate([high, low], axis=axis)


def halves(value):
    return value[:, :BLK] + value[:, BLK:]


def gram(both, turned):
    square = jnp.dot(turned, both, preferred_element_type=F32)
    return halves(square[:BLK] + square[BLK:])


def thirds(value):
    high = value.astype(BF16)
    rest = value - high.astype(F32)
    middle = rest.astype(BF16)
    return high, middle, (rest - middle.astype(F32)).astype(BF16)


def exact(a, b):
    ah, am, al = thirds(a)
    bh, bm, bl = thirds(b)
    left = jnp.concatenate([ah, am, ah, al], axis=1)
    near_zero = jnp.zeros_like(bl)
    right = jnp.concatenate(
        [
            jnp.concatenate([bh, bh, bl, bh], axis=0),
            jnp.concatenate([bm, bm, near_zero, near_zero], axis=0),
        ],
        axis=1,
    )
    return halves(jnp.dot(left, right, preferred_element_type=F32))


def lanes(shape):
    return lax.broadcasted_iota(jnp.int32, shape, 1)


def sublanes(shape):
    return lax.broadcasted_iota(jnp.int32, shape, 0)


def block(index):
    return slice(index * BLK, (index + 1) * BLK)


def present(m_ref, b, j):
    return m_ref[b, j].astype(F32)


def fetch(source, target, sem, parts):
    rows = source.shape[0] // parts
    copies = []
    for k in range(parts):
        part = pl.ds(k * rows, rows)
        copies.append(pltpu.make_async_copy(source.at[part], target.at[part], sem.at[k]))
        copies[-1].start()
    return copies


def arrive(copies):
    for copy in copies:
        copy.wait()


def only_present(m_ref, r_ref, blocks, columns, first, count):
    return jnp.concatenate(
        [
            jnp.concatenate(
                [
                    r_ref[block(b), pl.ds(pl.multiple_of(columns + k * BLK, BLK), BLK)]
                    * present(m_ref, b, first + k).astype(BF16)
                    for k in range(count)
                ],
                axis=1,
            )
            for b in blocks
        ],
        axis=0,
    )


def user_kernel(
    m_hbm, r_hbm, p_hbm, q_hbm, x_ref, m_ref, r_ref, p_ref, q_ref, qcat, grams, packed, r_sem, q_sem, p_sem, m_sem
):
    q_copies = fetch(q_hbm, q_ref, q_sem, 4)
    m_copy = pltpu.make_async_copy(m_hbm, m_ref, m_sem)
    m_copy.start()
    p_copies = fetch(p_hbm, p_ref, p_sem, 2)
    r_copies = fetch(r_hbm, r_ref, r_sem, UB)
    for j in range(IB):
        if j in (0, 3):
            arrive(q_copies[:1] if j == 0 else q_copies[1:])
        q = q_ref[block(j)]
        both = split(q, 1)
        qcat[block(j)] = both
        grams[j] = gram(both, split(q.T, 0))
    row64, lane64 = sublanes((64, BLK)), lanes((64, BLK))
    extra_row, extra_lane = sublanes((8, BLK)), lanes((8, BLK))
    extra = jnp.zeros((8, BLK), F32)
    arrive([m_copy] + p_copies + r_copies)
    for half in range(2):
        three = range(half * 3, half * 3 + 3)
        corrections = []
        for b in three:
            h = jnp.zeros((BLK, BLK), F32)
            count = jnp.int32(0)
            for j in range(IB):
                h = h + present(m_ref, b, j) * grams[j]
                count = count + m_ref[b, j]
            turned = jnp.concatenate([h[64:, 64:], h[64:, :64]], axis=1)
            packed[b * 64 : (b + 1) * 64] = jnp.where((lane64 < 64) & (lane64 > row64), turned, h[:64])
            diagonal = jnp.sum(jnp.where(lane64 == row64 + 64, h[64:], 0.0), axis=0, keepdims=True)
            if b % 2:
                diagonal = jnp.concatenate([diagonal[:, 64:], diagonal[:, :64]], axis=1)
            extra = extra + jnp.where(extra_row == b // 2, jnp.broadcast_to(diagonal, (8, BLK)), 0.0)
            extra = extra + jnp.where((extra_row == 3) & (extra_lane == b), count.astype(F32), 0.0)
            corrections.append(exact(p_ref[block(b)], h))
        masked = only_present(m_ref, r_ref, three, 0, 0, IB)
        found = halves(jnp.dot(masked, qcat[...], preferred_element_type=F32))
        d = found - jnp.concatenate(corrections, axis=0)
        for k in range(8 * ROWS // 4):
            x_ref[half * 8 + k // 12, k % 12] = d[k * 4 : (k + 1) * 4]
    for piece in range(PIECES):
        for k in range(HROWS // 4):
            x_ref[piece, ROWS // 4 + k] = packed[piece * HROWS + k * 4 : piece * HROWS + (k + 1) * 4]
        x_ref[piece, SENT // 4] = extra[:4]


def total_kernel(y_ref, z_ref, extra_ref, rows):
    for k in range(TILES):
        total = y_ref[0, k]
        for piece in range(1, PIECES):
            total = total + y_ref[piece, k]
        rows[k * 4 : (k + 1) * 4] = total
    extra_ref[...] = rows[SENT : SENT + 8]
    total = rows[:SENT]
    for piece in range(PIECES):
        z_ref[piece] = total


def item_kernel(
    m_ref, step_ref, r_ref, p_ref, q_ref, z_ref, extra_ref, new_ref, other_ref, turned_ref, grams
):
    extra = extra_ref[...]
    scales = step_ref[0] / (BLK * (1.0 + extra[3:4]))
    flipped = jnp.concatenate([extra[:, 64:], extra[:, :64]], axis=1)
    row64, lane64 = sublanes((64, BLK)), lanes((64, BLK))
    for b in range(UB):
        tiles = []
        for k in range(0, BLK, 16):
            piece, at = divmod(b * BLK + k, ROWS)
            tiles.append(z_ref[piece, at : at + 16])
        d = jnp.concatenate(tiles, axis=0)
        tiles = []
        for k in range(0, 64, 8):
            piece, at = divmod(b * 64 + k, HROWS)
            tiles.append(z_ref[piece, ROWS + at : ROWS + at + 8])
        half = jnp.concatenate(tiles, axis=0)
        turned = jnp.concatenate([half[:, 64:], half[:, :64]], axis=1)
        top = jnp.where(lane64 < row64, half, jnp.where(lane64 == row64, 0.5 * half, 0.0))
        top = jnp.where(lane64 >= 64, half, top)
        bottom = jnp.where(lane64 > row64 + 64, turned, 0.0)
        bottom = jnp.where(lane64 == row64 + 64, 0.5 * (flipped if b % 2 else extra)[b // 2 : b // 2 + 1], bottom)
        w = jnp.concatenate([top, bottom], axis=0)
        s = scales[:, b : b + 1]
        new = p_ref[block(b)] + (2.0 * s) * d - (s * s) * exact(d, w + w.T)
        new_ref[block(b)] = new
        turned = split(new.T, 0)
        turned_ref[:, block(b)] = turned
        grams[b] = gram(split(new, 1), turned)
    core = lax.rem(lax.axis_index("user"), 2)
    item_half(1 - core, m_ref, step_ref, r_ref, q_ref, turned_ref, grams, other_ref)


def item_half(side, m_ref, step_ref, r_ref, q_ref, turned_ref, grams, o_ref):
    counts = jnp.zeros((8, BLK), F32)
    row8, lane8 = sublanes((8, BLK)), lanes((8, BLK))
    for j in range(IB):
        count = jnp.int32(0)
        for b in range(UB):
            count = count + m_ref[b, j]
        counts = counts + jnp.where(lane8 == j, count.astype(F32), 0.0)
    step = jnp.where(lax.axis_index("user") == 0, step_ref[1], 0.0)
    counts = jnp.where(row8 == 0, counts, step)
    first = side * (IB // 2)
    for pair in range(IB // 4):
        columns = pl.multiple_of(side * (ITEMS // 2) + pair * 2 * BLK, BLK)
        masked = only_present(m_ref, r_ref, range(UB), columns, first + pair * 2, 2)
        found = jnp.dot(turned_ref[...], masked, preferred_element_type=F32)
        found = found[:BLK] + found[BLK:]
        for k in range(2):
            s = jnp.zeros((BLK, BLK), F32)
            for b in range(UB):
                s = s + present(m_ref, b, first + pair * 2 + k) * grams[b]
            q = q_ref[pl.ds(pl.multiple_of(columns + k * BLK, BLK), BLK)]
            grad = found[:, block(k)].T - exact(q, s)
            for part in range(4):
                piece, at = divmod((pair * 2 + k) * 4 + part, 3)
                o_ref[piece, at * 32 : (at + 1) * 32] = grad[part * 32 : (part + 1) * 32]
    for piece in range(8):
        o_ref[piece, CHUNK:] = counts


def own_kernel(m_ref, step_ref, r_ref, q_ref, turned_ref, grams, new_ref, own_ref, o_hbm, sem):
    copies = fetch(new_ref, o_hbm, sem, 2)
    core = lax.rem(lax.axis_index("user"), 2)
    item_half(core, m_ref, step_ref, r_ref, q_ref, turned_ref, grams, own_ref)
    arrive(copies)


def scale_kernel(v_ref, q_ref, o_ref):
    user = lax.axis_index("user")
    total = v_ref[0]
    for k in range(1, 8):
        total = total + v_ref[k]
    scales = total[CHUNK + 1 : CHUNK + 2] / (BLK * (1.0 + total[CHUNK : CHUNK + 1]))
    lane1 = lanes((1, BLK))
    for k in range(3):
        place = lax.rem(user, 2) * 24 + (user // 2) * 3 + k
        t = jnp.sum(jnp.where(lane1 == place // 4, scales, 0.0), axis=1, keepdims=True)
        start = pl.multiple_of(place * 32, 8)
        new = q_ref[pl.ds(start, 32)] + t * total[k * 32 : (k + 1) * 32]
        for piece in range(8):
            o_ref[piece, k * 32 : (k + 1) * 32] = new


def place_kernel(flip, half_ref, whole, o_hbm, sem):
    core = lax.rem(lax.axis_index("user"), 2)
    side = 1 - core if flip else core
    copies = []
    for k in range(4):
        rows = pl.ds(pl.multiple_of(side * (ITEMS // 2) + k * 192, 8), 192)
        copies.append(pltpu.make_async_copy(half_ref.at[pl.ds(k * 192, 192)], o_hbm.at[rows], sem.at[k]))
        copies[-1].start()
    arrive(copies)


def place_own_kernel(half_ref, o_hbm, sem):
    place_kernel(False, half_ref, None, o_hbm, sem)


def place_other_kernel(half_ref, whole, o_hbm, sem):
    place_kernel(True, half_ref, whole, o_hbm, sem)


def near(value):
    return pltpu.with_memory_space_constraint(value, pltpu.VMEM)


def far(value):
    return pltpu.with_memory_space_constraint(value, pltpu.HBM)


def call(kernel, out_shapes, specs, scratch=(), limit=8, out_specs=VMEM, cost=None, alias={}):
    single = len(out_shapes) == 1
    return pl.pallas_call(
        kernel,
        out_shape=out_shapes[0] if single else out_shapes,
        in_specs=specs,
        out_specs=out_specs if single or isinstance(out_specs, list) else [out_specs] * len(out_shapes),
        scratch_shapes=scratch,
        compiler_params=pltpu.CompilerParams(vmem_limit_bytes=limit << 20),
        cost_estimate=cost,
        input_output_aliases=alias,
    )


def body(ratings, presence, user_factors, item_factors, step_sizes):
    swap = [(k, k ^ 1) for k in range(16)]
    chips = [[k + 2 * j for j in range(8)] for k in range(2)]
    x = call(
        user_kernel,
        [pltpu.VMEM((PIECES, TILES, 4, BLK), F32)],
        [HBM, HBM, HBM, HBM],
        [
            pltpu.SMEM((UB, IB), jnp.int32),
            pltpu.VMEM((USERS, ITEMS), BF16),
            pltpu.VMEM((USERS, BLK), F32),
            pltpu.VMEM((ITEMS, BLK), F32),
            pltpu.VMEM((ITEMS, 2 * BLK), BF16),
            pltpu.VMEM((IB, BLK, BLK), F32),
            pltpu.VMEM((UB * 64, BLK), F32),
            pltpu.SemaphoreType.DMA((UB,)),
            pltpu.SemaphoreType.DMA((4,)),
            pltpu.SemaphoreType.DMA((2,)),
            pltpu.SemaphoreType.DMA,
        ],
        limit=16,
    )(far(presence), far(ratings), far(user_factors), far(item_factors))
    y = lax.all_to_all(x, "item", 0, 0, tiled=True)
    z, extra = call(
        total_kernel,
        [pltpu.VMEM((PIECES, SENT, BLK), F32), pltpu.VMEM((8, BLK), F32)],
        [VMEM],
        [pltpu.VMEM((SENT + 8, BLK), F32)],
    )(near(y))
    z = lax.all_to_all(z, "item", 0, 0, tiled=True)
    new, other, turned, grams = call(
        item_kernel,
        [
            pltpu.VMEM((USERS, BLK), F32),
            pltpu.VMEM((8, CHUNK + 8, BLK), F32),
            pltpu.VMEM((2 * BLK, USERS), BF16),
            pltpu.VMEM((UB, BLK, BLK), F32),
        ],
        [SMEM, SMEM, VMEM, VMEM, VMEM, VMEM, VMEM],
        limit=16,
    )(presence, step_sizes, near(ratings), near(user_factors), near(item_factors), near(z), near(extra))
    received = lax.ppermute(other, "user", swap)
    own, new_users = call(
        own_kernel,
        [pltpu.VMEM((8, CHUNK + 8, BLK), F32), pltpu.HBM((USERS, BLK), F32)],
        [SMEM, SMEM, VMEM, VMEM, VMEM, VMEM, VMEM],
        [pltpu.SemaphoreType.DMA((2,))],
        limit=16,
        out_specs=[VMEM, HBM],
        cost=pl.CostEstimate(flops=1 << 32, bytes_accessed=1 << 23, transcendentals=0),
    )(presence, step_sizes, near(ratings), near(item_factors), near(turned), near(grams), near(new))
    v = own + received
    v = lax.all_to_all(v, "user", 0, 0, tiled=True, axis_index_groups=chips)
    owned = call(scale_kernel, [pltpu.VMEM((8, CHUNK, BLK), F32)], [VMEM, VMEM])(
        near(v), near(item_factors)
    )
    mine = lax.all_to_all(owned, "user", 0, 0, tiled=True, axis_index_groups=chips)
    theirs = lax.ppermute(mine, "user", swap)
    half = call(
        place_own_kernel,
        [pltpu.HBM((ITEMS, BLK), F32)],
        [VMEM],
        [pltpu.SemaphoreType.DMA((4,))],
        out_specs=HBM,
        cost=pl.CostEstimate(flops=1 << 30, bytes_accessed=1 << 22, transcendentals=0),
    )(near(mine.reshape(ITEMS // 2, BLK)))
    new_items = call(
        place_other_kernel,
        [pltpu.HBM((ITEMS, BLK), F32)],
        [VMEM, HBM],
        [pltpu.SemaphoreType.DMA((4,))],
        out_specs=HBM,
        alias={1: 0},
    )(near(theirs.reshape(ITEMS // 2, BLK)), half)
    return new_users, new_items


def solution(mesh):
    return jax.shard_map(
        body,
        mesh=mesh,
        in_specs=(P("user", "item"), P("user", "item"), P("user", None), P("item", None), P()),
        out_specs=(P("user", None), P("item", None)),
        check_vma=False,
    )
```

```python
import jax
import jax.numpy as jnp
from jax import lax
from jax.experimental import pallas as pl
from jax.experimental.pallas import tpu as pltpu
from jax.sharding import PartitionSpec as P

BLK = 128
UB = 6
IB = 12
USERS = UB * BLK
ITEMS = IB * BLK
PIECES = 16
ROWS = USERS // PIECES
HROWS = UB * 64 // PIECES
SENT = ROWS + HROWS
TILES = SENT // 4 + 1
CHUNK = ITEMS // 16
F32 = jnp.float32
BF16 = jnp.bfloat16
VMEM = pl.BlockSpec(memory_space=pltpu.VMEM)
SMEM = pl.BlockSpec(memory_space=pltpu.SMEM)
HBM = pl.BlockSpec(memory_space=pltpu.HBM)


def split(value, axis):
    high = value.astype(BF16)
    low = (value - high.astype(F32)).astype(BF16)
    return jnp.concatenate([high, low], axis=axis)


def halves(value):
    return value[:, :BLK] + value[:, BLK:]


def gram(both, turned):
    square = jnp.dot(turned, both, preferred_element_type=F32)
    return halves(square[:BLK] + square[BLK:])


def thirds(value):
    high = value.astype(BF16)
    rest = value - high.astype(F32)
    middle = rest.astype(BF16)
    return high, middle, (rest - middle.astype(F32)).astype(BF16)


def exact(a, b):
    ah, am, al = thirds(a)
    bh, bm, bl = thirds(b)
    left = jnp.concatenate([ah, am, ah, al], axis=1)
    near_zero = jnp.zeros_like(bl)
    right = jnp.concatenate(
        [
            jnp.concatenate([bh, bh, bl, bh], axis=0),
            jnp.concatenate([bm, bm, near_zero, near_zero], axis=0),
        ],
        axis=1,
    )
    return halves(jnp.dot(left, right, preferred_element_type=F32))


def lanes(shape):
    return lax.broadcasted_iota(jnp.int32, shape, 1)


def sublanes(shape):
    return lax.broadcasted_iota(jnp.int32, shape, 0)


def block(index):
    return slice(index * BLK, (index + 1) * BLK)


def present(m_ref, b, j):
    return m_ref[b, j].astype(F32)


def fetch(source, target, sem, parts):
    rows = source.shape[0] // parts
    copies = []
    for k in range(parts):
        part = pl.ds(k * rows, rows)
        copies.append(pltpu.make_async_copy(source.at[part], target.at[part], sem.at[k]))
        copies[-1].start()
    return copies


def arrive(copies):
    for copy in copies:
        copy.wait()


def only_present(m_ref, r_ref, blocks, columns, first, count):
    return jnp.concatenate(
        [
            jnp.concatenate(
                [
                    r_ref[block(b), pl.ds(pl.multiple_of(columns + k * BLK, BLK), BLK)]
                    * present(m_ref, b, first + k).astype(BF16)
                    for k in range(count)
                ],
                axis=1,
            )
            for b in blocks
        ],
        axis=0,
    )


def user_kernel(
    m_hbm, r_hbm, p_hbm, q_hbm, x_ref, m_ref, r_ref, p_ref, q_ref, qcat, grams, packed, r_sem, q_sem, p_sem, m_sem
):
    q_copies = fetch(q_hbm, q_ref, q_sem, 4)
    m_copy = pltpu.make_async_copy(m_hbm, m_ref, m_sem)
    m_copy.start()
    p_copies = fetch(p_hbm, p_ref, p_sem, 2)
    r_copies = fetch(r_hbm, r_ref, r_sem, UB)
    for j in range(IB):
        if j in (0, 3):
            arrive(q_copies[:1] if j == 0 else q_copies[1:])
        q = q_ref[block(j)]
        both = split(q, 1)
        qcat[block(j)] = both
        grams[j] = gram(both, split(q.T, 0))
    row64, lane64 = sublanes((64, BLK)), lanes((64, BLK))
    extra_row, extra_lane = sublanes((8, BLK)), lanes((8, BLK))
    extra = jnp.zeros((8, BLK), F32)
    arrive([m_copy] + p_copies + r_copies)
    masked = only_present(m_ref, r_ref, range(UB), 0, 0, IB)
    found = halves(jnp.dot(masked, qcat[...], preferred_element_type=F32))
    corrections = []
    for b in range(UB):
        h = jnp.zeros((BLK, BLK), F32)
        count = jnp.int32(0)
        for j in range(IB):
            h = h + present(m_ref, b, j) * grams[j]
            count = count + m_ref[b, j]
        turned = jnp.concatenate([h[64:, 64:], h[64:, :64]], axis=1)
        packed[b * 64 : (b + 1) * 64] = jnp.where((lane64 < 64) & (lane64 > row64), turned, h[:64])
        diagonal = jnp.sum(jnp.where(lane64 == row64 + 64, h[64:], 0.0), axis=0, keepdims=True)
        if b % 2:
            diagonal = jnp.concatenate([diagonal[:, 64:], diagonal[:, :64]], axis=1)
        extra = extra + jnp.where(extra_row == b // 2, jnp.broadcast_to(diagonal, (8, BLK)), 0.0)
        extra = extra + jnp.where((extra_row == 3) & (extra_lane == b), count.astype(F32), 0.0)
        corrections.append(exact(p_ref[block(b)], h))
    d = found - jnp.concatenate(corrections, axis=0)
    for k in range(PIECES * ROWS // 4):
        x_ref[k // 12, k % 12] = d[k * 4 : (k + 1) * 4]
    for piece in range(PIECES):
        for k in range(HROWS // 4):
            x_ref[piece, ROWS // 4 + k] = packed[piece * HROWS + k * 4 : piece * HROWS + (k + 1) * 4]
        x_ref[piece, SENT // 4] = extra[:4]


def total_kernel(y_ref, z_ref, extra_ref, rows):
    for k in range(TILES):
        total = y_ref[0, k]
        for piece in range(1, PIECES):
            total = total + y_ref[piece, k]
        rows[k * 4 : (k + 1) * 4] = total
    extra_ref[...] = rows[SENT : SENT + 8]
    total = rows[:SENT]
    for piece in range(PIECES):
        z_ref[piece] = total


def item_kernel(
    m_ref, step_ref, r_ref, p_ref, q_ref, z_ref, extra_ref, new_ref, other_ref, turned_ref, grams
):
    extra = extra_ref[...]
    scales = step_ref[0] / (BLK * (1.0 + extra[3:4]))
    flipped = jnp.concatenate([extra[:, 64:], extra[:, :64]], axis=1)
    row64, lane64 = sublanes((64, BLK)), lanes((64, BLK))
    for b in range(UB):
        tiles = []
        for k in range(0, BLK, 16):
            piece, at = divmod(b * BLK + k, ROWS)
            tiles.append(z_ref[piece, at : at + 16])
        d = jnp.concatenate(tiles, axis=0)
        tiles = []
        for k in range(0, 64, 8):
            piece, at = divmod(b * 64 + k, HROWS)
            tiles.append(z_ref[piece, ROWS + at : ROWS + at + 8])
        half = jnp.concatenate(tiles, axis=0)
        turned = jnp.concatenate([half[:, 64:], half[:, :64]], axis=1)
        top = jnp.where(lane64 < row64, half, jnp.where(lane64 == row64, 0.5 * half, 0.0))
        top = jnp.where(lane64 >= 64, half, top)
        bottom = jnp.where(lane64 > row64 + 64, turned, 0.0)
        bottom = jnp.where(lane64 == row64 + 64, 0.5 * (flipped if b % 2 else extra)[b // 2 : b // 2 + 1], bottom)
        w = jnp.concatenate([top, bottom], axis=0)
        s = scales[:, b : b + 1]
        new = p_ref[block(b)] + (2.0 * s) * d - (s * s) * exact(d, w + w.T)
        new_ref[block(b)] = new
        turned = split(new.T, 0)
        turned_ref[:, block(b)] = turned
        grams[b] = gram(split(new, 1), turned)
    core = lax.rem(lax.axis_index("user"), 2)
    item_half(1 - core, m_ref, step_ref, r_ref, q_ref, turned_ref, grams, other_ref)


def item_half(side, m_ref, step_ref, r_ref, q_ref, turned_ref, grams, o_ref):
    counts = jnp.zeros((8, BLK), F32)
    row8, lane8 = sublanes((8, BLK)), lanes((8, BLK))
    for j in range(IB):
        count = jnp.int32(0)
        for b in range(UB):
            count = count + m_ref[b, j]
        counts = counts + jnp.where(lane8 == j, count.astype(F32), 0.0)
    step = jnp.where(lax.axis_index("user") == 0, step_ref[1], 0.0)
    counts = jnp.where(row8 == 0, counts, step)
    first = side * (IB // 2)
    for pair in range(IB // 4):
        columns = pl.multiple_of(side * (ITEMS // 2) + pair * 2 * BLK, BLK)
        masked = only_present(m_ref, r_ref, range(UB), columns, first + pair * 2, 2)
        found = jnp.dot(turned_ref[...], masked, preferred_element_type=F32)
        found = found[:BLK] + found[BLK:]
        for k in range(2):
            s = jnp.zeros((BLK, BLK), F32)
            for b in range(UB):
                s = s + present(m_ref, b, first + pair * 2 + k) * grams[b]
            q = q_ref[pl.ds(pl.multiple_of(columns + k * BLK, BLK), BLK)]
            grad = found[:, block(k)].T - exact(q, s)
            for part in range(4):
                piece, at = divmod((pair * 2 + k) * 4 + part, 3)
                o_ref[piece, at * 32 : (at + 1) * 32] = grad[part * 32 : (part + 1) * 32]
    for piece in range(8):
        o_ref[piece, CHUNK:] = counts


def own_kernel(m_ref, step_ref, r_ref, q_ref, turned_ref, grams, own_ref):
    core = lax.rem(lax.axis_index("user"), 2)
    item_half(core, m_ref, step_ref, r_ref, q_ref, turned_ref, grams, own_ref)


def scale_kernel(v_ref, q_ref, o_ref):
    user = lax.axis_index("user")
    total = v_ref[0]
    for k in range(1, 8):
        total = total + v_ref[k]
    scales = total[CHUNK + 1 : CHUNK + 2] / (BLK * (1.0 + total[CHUNK : CHUNK + 1]))
    lane1 = lanes((1, BLK))
    for k in range(3):
        place = lax.rem(user, 2) * 24 + (user // 2) * 3 + k
        t = jnp.sum(jnp.where(lane1 == place // 4, scales, 0.0), axis=1, keepdims=True)
        start = pl.multiple_of(place * 32, 8)
        new = q_ref[pl.ds(start, 32)] + t * total[k * 32 : (k + 1) * 32]
        for piece in range(8):
            o_ref[piece, k * 32 : (k + 1) * 32] = new


def place(side, half_ref, o_hbm, sem):
    copies = []
    for k in range(4):
        rows = pl.ds(pl.multiple_of(side * (ITEMS // 2) + k * 192, 8), 192)
        copies.append(pltpu.make_async_copy(half_ref.at[pl.ds(k * 192, 192)], o_hbm.at[rows], sem.at[k]))
        copies[-1].start()
    return copies


def place_own_kernel(half_ref, new_ref, o_hbm, new_hbm, sem, new_sem):
    core = lax.rem(lax.axis_index("user"), 2)
    arrive(place(core, half_ref, o_hbm, sem) + fetch(new_ref, new_hbm, new_sem, 4))


def place_other_kernel(half_ref, whole, o_hbm, sem):
    core = lax.rem(lax.axis_index("user"), 2)
    arrive(place(1 - core, half_ref, o_hbm, sem))


def near(value):
    return pltpu.with_memory_space_constraint(value, pltpu.VMEM)


def far(value):
    return pltpu.with_memory_space_constraint(value, pltpu.HBM)


def call(kernel, out_shapes, specs, scratch=(), limit=8, out_specs=VMEM, cost=None, alias={}):
    single = len(out_shapes) == 1
    return pl.pallas_call(
        kernel,
        out_shape=out_shapes[0] if single else out_shapes,
        in_specs=specs,
        out_specs=out_specs if single or isinstance(out_specs, list) else [out_specs] * len(out_shapes),
        scratch_shapes=scratch,
        compiler_params=pltpu.CompilerParams(vmem_limit_bytes=limit << 20),
        cost_estimate=cost,
        input_output_aliases=alias,
    )


def body(ratings, presence, user_factors, item_factors, step_sizes):
    swap = [(k, k ^ 1) for k in range(16)]
    chips = [[k + 2 * j for j in range(8)] for k in range(2)]
    x = call(
        user_kernel,
        [pltpu.VMEM((PIECES, TILES, 4, BLK), F32)],
        [HBM, HBM, HBM, HBM],
        [
            pltpu.SMEM((UB, IB), jnp.int32),
            pltpu.VMEM((USERS, ITEMS), BF16),
            pltpu.VMEM((USERS, BLK), F32),
            pltpu.VMEM((ITEMS, BLK), F32),
            pltpu.VMEM((ITEMS, 2 * BLK), BF16),
            pltpu.VMEM((IB, BLK, BLK), F32),
            pltpu.VMEM((UB * 64, BLK), F32),
            pltpu.SemaphoreType.DMA((UB,)),
            pltpu.SemaphoreType.DMA((4,)),
            pltpu.SemaphoreType.DMA((2,)),
            pltpu.SemaphoreType.DMA,
        ],
        limit=16,
    )(far(presence), far(ratings), far(user_factors), far(item_factors))
    y = lax.all_to_all(x, "item", 0, 0, tiled=True)
    z, extra = call(
        total_kernel,
        [pltpu.VMEM((PIECES, SENT, BLK), F32), pltpu.VMEM((8, BLK), F32)],
        [VMEM],
        [pltpu.VMEM((SENT + 8, BLK), F32)],
    )(near(y))
    z = lax.all_to_all(z, "item", 0, 0, tiled=True)
    new, other, turned, grams = call(
        item_kernel,
        [
            pltpu.VMEM((USERS, BLK), F32),
            pltpu.VMEM((8, CHUNK + 8, BLK), F32),
            pltpu.VMEM((2 * BLK, USERS), BF16),
            pltpu.VMEM((UB, BLK, BLK), F32),
        ],
        [SMEM, SMEM, VMEM, VMEM, VMEM, VMEM, VMEM],
        limit=16,
    )(presence, step_sizes, near(ratings), near(user_factors), near(item_factors), near(z), near(extra))
    received = lax.ppermute(other, "user", swap)
    own = call(
        own_kernel,
        [pltpu.VMEM((8, CHUNK + 8, BLK), F32)],
        [SMEM, SMEM, VMEM, VMEM, VMEM, VMEM],
        limit=16,
        cost=pl.CostEstimate(flops=1 << 32, bytes_accessed=1 << 23, transcendentals=0),
    )(presence, step_sizes, near(ratings), near(item_factors), near(turned), near(grams))
    v = own + received
    v = lax.all_to_all(v, "user", 0, 0, tiled=True, axis_index_groups=chips)
    owned = call(scale_kernel, [pltpu.VMEM((8, CHUNK, BLK), F32)], [VMEM, VMEM])(
        near(v), near(item_factors)
    )
    mine = lax.all_to_all(owned, "user", 0, 0, tiled=True, axis_index_groups=chips)
    theirs = lax.ppermute(mine, "user", swap)
    half, new_users = call(
        place_own_kernel,
        [pltpu.HBM((ITEMS, BLK), F32), pltpu.HBM((USERS, BLK), F32)],
        [VMEM, VMEM],
        [pltpu.SemaphoreType.DMA((4,)), pltpu.SemaphoreType.DMA((4,))],
        out_specs=HBM,
        cost=pl.CostEstimate(flops=1 << 30, bytes_accessed=1 << 22, transcendentals=0),
    )(near(mine.reshape(ITEMS // 2, BLK)), near(new))
    new_items = call(
        place_other_kernel,
        [pltpu.HBM((ITEMS, BLK), F32)],
        [VMEM, HBM],
        [pltpu.SemaphoreType.DMA((4,))],
        out_specs=HBM,
        alias={1: 0},
    )(near(theirs.reshape(ITEMS // 2, BLK)), half)
    return new_users, new_items


def solution(mesh):
    return jax.shard_map(
        body,
        mesh=mesh,
        in_specs=(P("user", "item"), P("user", "item"), P("user", None), P("item", None), P()),
        out_specs=(P("user", None), P("item", None)),
        check_vma=False,
    )
```

```python
import jax
import jax.numpy as jnp
from jax import lax
from jax.experimental import pallas as pl
from jax.experimental.pallas import tpu as pltpu
from jax.sharding import PartitionSpec as P

BLK = 128
UB = 6
IB = 12
USERS = UB * BLK
ITEMS = IB * BLK
PIECES = 16
ROWS = USERS // PIECES
HROWS = UB * 64 // PIECES
SENT = ROWS + HROWS
TILES = SENT // 4 + 1
CHUNK = ITEMS // 16
F32 = jnp.float32
BF16 = jnp.bfloat16
VMEM = pl.BlockSpec(memory_space=pltpu.VMEM)
SMEM = pl.BlockSpec(memory_space=pltpu.SMEM)
HBM = pl.BlockSpec(memory_space=pltpu.HBM)


def split(value, axis):
    high = value.astype(BF16)
    low = (value - high.astype(F32)).astype(BF16)
    return jnp.concatenate([high, low], axis=axis)


def halves(value):
    return value[:, :BLK] + value[:, BLK:]


def gram(both, turned):
    square = jnp.dot(turned, both, preferred_element_type=F32)
    return halves(square[:BLK] + square[BLK:])


def thirds(value):
    high = value.astype(BF16)
    rest = value - high.astype(F32)
    middle = rest.astype(BF16)
    return high, middle, (rest - middle.astype(F32)).astype(BF16)


def exact(a, b):
    ah, am, al = thirds(a)
    bh, bm, bl = thirds(b)
    left = jnp.concatenate([ah, am, ah, al], axis=1)
    near_zero = jnp.zeros_like(bl)
    right = jnp.concatenate(
        [
            jnp.concatenate([bh, bh, bl, bh], axis=0),
            jnp.concatenate([bm, bm, near_zero, near_zero], axis=0),
        ],
        axis=1,
    )
    return halves(jnp.dot(left, right, preferred_element_type=F32))


def lanes(shape):
    return lax.broadcasted_iota(jnp.int32, shape, 1)


def sublanes(shape):
    return lax.broadcasted_iota(jnp.int32, shape, 0)


def block(index):
    return slice(index * BLK, (index + 1) * BLK)


def present(m_ref, b, j):
    return m_ref[b, j].astype(F32)


def fetch(source, target, sem, parts):
    rows = source.shape[0] // parts
    copies = []
    for k in range(parts):
        part = pl.ds(k * rows, rows)
        copies.append(pltpu.make_async_copy(source.at[part], target.at[part], sem.at[k]))
        copies[-1].start()
    return copies


def arrive(copies):
    for copy in copies:
        copy.wait()


def only_present(m_ref, r_ref, blocks, columns, first, count):
    return jnp.concatenate(
        [
            jnp.concatenate(
                [
                    r_ref[block(b), pl.ds(pl.multiple_of(columns + k * BLK, BLK), BLK)]
                    * present(m_ref, b, first + k).astype(BF16)
                    for k in range(count)
                ],
                axis=1,
            )
            for b in blocks
        ],
        axis=0,
    )


def user_kernel(
    m_hbm, r_hbm, p_hbm, q_hbm, x_ref, m_ref, r_ref, p_ref, q_ref, qcat, turned, grams, packed, r_sem, q_sem, p_sem, m_sem
):
    q_copies = fetch(q_hbm, q_ref, q_sem, 4)
    m_copy = pltpu.make_async_copy(m_hbm, m_ref, m_sem)
    m_copy.start()
    p_copies = fetch(p_hbm, p_ref, p_sem, 2)
    r_copies = fetch(r_hbm, r_ref, r_sem, UB)
    for j in range(IB):
        if j in (0, 3):
            arrive(q_copies[:1] if j == 0 else q_copies[1:])
        q = q_ref[block(j)]
        qcat[block(j)] = split(q, 1)
        turned[j] = split(q.T, 0)
    for j in range(IB):
        grams[j] = gram(qcat[block(j)], turned[j])
    row64, lane64 = sublanes((64, BLK)), lanes((64, BLK))
    extra_row, extra_lane = sublanes((8, BLK)), lanes((8, BLK))
    extra = jnp.zeros((8, BLK), F32)
    arrive([m_copy] + p_copies + r_copies)
    masked = only_present(m_ref, r_ref, range(UB), 0, 0, IB)
    found = halves(jnp.dot(masked, qcat[...], preferred_element_type=F32))
    corrections = []
    for b in range(UB):
        h = jnp.zeros((BLK, BLK), F32)
        count = jnp.int32(0)
        for j in range(IB):
            h = h + present(m_ref, b, j) * grams[j]
            count = count + m_ref[b, j]
        moved = jnp.concatenate([h[64:, 64:], h[64:, :64]], axis=1)
        packed[b * 64 : (b + 1) * 64] = jnp.where((lane64 < 64) & (lane64 > row64), moved, h[:64])
        diagonal = jnp.sum(jnp.where(lane64 == row64 + 64, h[64:], 0.0), axis=0, keepdims=True)
        if b % 2:
            diagonal = jnp.concatenate([diagonal[:, 64:], diagonal[:, :64]], axis=1)
        extra = extra + jnp.where(extra_row == b // 2, jnp.broadcast_to(diagonal, (8, BLK)), 0.0)
        extra = extra + jnp.where((extra_row == 3) & (extra_lane == b), count.astype(F32), 0.0)
        corrections.append(exact(p_ref[block(b)], h))
    d = found - jnp.concatenate(corrections, axis=0)
    for k in range(PIECES * ROWS // 4):
        x_ref[k // 12, k % 12] = d[k * 4 : (k + 1) * 4]
    for piece in range(PIECES):
        for k in range(HROWS // 4):
            x_ref[piece, ROWS // 4 + k] = packed[piece * HROWS + k * 4 : piece * HROWS + (k + 1) * 4]
        x_ref[piece, SENT // 4] = extra[:4]


def total_kernel(y_ref, z_ref, extra_ref, rows):
    for k in range(TILES):
        total = y_ref[0, k]
        for piece in range(1, PIECES):
            total = total + y_ref[piece, k]
        rows[k * 4 : (k + 1) * 4] = total
    extra_ref[...] = rows[SENT : SENT + 8]
    total = rows[:SENT]
    for piece in range(PIECES):
        z_ref[piece] = total


def item_kernel(
    m_ref, step_ref, r_ref, p_ref, q_ref, z_ref, extra_ref, new_ref, other_ref, turned_ref, grams
):
    extra = extra_ref[...]
    scales = step_ref[0] / (BLK * (1.0 + extra[3:4]))
    flipped = jnp.concatenate([extra[:, 64:], extra[:, :64]], axis=1)
    row64, lane64 = sublanes((64, BLK)), lanes((64, BLK))
    for b in range(UB):
        tiles = []
        for k in range(0, BLK, 16):
            piece, at = divmod(b * BLK + k, ROWS)
            tiles.append(z_ref[piece, at : at + 16])
        d = jnp.concatenate(tiles, axis=0)
        tiles = []
        for k in range(0, 64, 8):
            piece, at = divmod(b * 64 + k, HROWS)
            tiles.append(z_ref[piece, ROWS + at : ROWS + at + 8])
        half = jnp.concatenate(tiles, axis=0)
        turned = jnp.concatenate([half[:, 64:], half[:, :64]], axis=1)
        top = jnp.where(lane64 < row64, half, jnp.where(lane64 == row64, 0.5 * half, 0.0))
        top = jnp.where(lane64 >= 64, half, top)
        bottom = jnp.where(lane64 > row64 + 64, turned, 0.0)
        bottom = jnp.where(lane64 == row64 + 64, 0.5 * (flipped if b % 2 else extra)[b // 2 : b // 2 + 1], bottom)
        w = jnp.concatenate([top, bottom], axis=0)
        s = scales[:, b : b + 1]
        new = p_ref[block(b)] + (2.0 * s) * d - (s * s) * exact(d, w + w.T)
        new_ref[block(b)] = new
    for b in range(UB):
        new = new_ref[block(b)]
        turned = split(new.T, 0)
        turned_ref[:, block(b)] = turned
        grams[b] = gram(split(new, 1), turned)
    core = lax.rem(lax.axis_index("user"), 2)
    item_half(1 - core, m_ref, step_ref, r_ref, q_ref, turned_ref, grams, other_ref)


def item_half(side, m_ref, step_ref, r_ref, q_ref, turned_ref, grams, o_ref):
    counts = jnp.zeros((8, BLK), F32)
    row8, lane8 = sublanes((8, BLK)), lanes((8, BLK))
    for j in range(IB):
        count = jnp.int32(0)
        for b in range(UB):
            count = count + m_ref[b, j]
        counts = counts + jnp.where(lane8 == j, count.astype(F32), 0.0)
    step = jnp.where(lax.axis_index("user") == 0, step_ref[1], 0.0)
    counts = jnp.where(row8 == 0, counts, step)
    first = side * (IB // 2)
    columns = pl.multiple_of(side * (ITEMS // 2), BLK)
    masked = only_present(m_ref, r_ref, range(UB), columns, first, IB // 2)
    found = jnp.dot(turned_ref[...], masked, preferred_element_type=F32)
    found = found[:BLK] + found[BLK:]
    for k in range(IB // 2):
        s = jnp.zeros((BLK, BLK), F32)
        for b in range(UB):
            s = s + present(m_ref, b, first + k) * grams[b]
        q = q_ref[pl.ds(pl.multiple_of(columns + k * BLK, BLK), BLK)]
        grad = found[:, block(k)].T - exact(q, s)
        for part in range(4):
            piece, at = divmod(k * 4 + part, 3)
            o_ref[piece, at * 32 : (at + 1) * 32] = grad[part * 32 : (part + 1) * 32]
    for piece in range(8):
        o_ref[piece, CHUNK:] = counts


def own_kernel(m_ref, step_ref, r_ref, q_ref, turned_ref, grams, own_ref):
    core = lax.rem(lax.axis_index("user"), 2)
    item_half(core, m_ref, step_ref, r_ref, q_ref, turned_ref, grams, own_ref)


def scale_kernel(v_ref, q_ref, o_ref):
    user = lax.axis_index("user")
    total = v_ref[0]
    for k in range(1, 8):
        total = total + v_ref[k]
    scales = total[CHUNK + 1 : CHUNK + 2] / (BLK * (1.0 + total[CHUNK : CHUNK + 1]))
    lane1 = lanes((1, BLK))
    for k in range(3):
        place = lax.rem(user, 2) * 24 + (user // 2) * 3 + k
        t = jnp.sum(jnp.where(lane1 == place // 4, scales, 0.0), axis=1, keepdims=True)
        start = pl.multiple_of(place * 32, 8)
        new = q_ref[pl.ds(start, 32)] + t * total[k * 32 : (k + 1) * 32]
        for piece in range(8):
            o_ref[piece, k * 32 : (k + 1) * 32] = new


def place(side, half_ref, o_hbm, sem):
    copies = []
    for k in range(4):
        rows = pl.ds(pl.multiple_of(side * (ITEMS // 2) + k * 192, 8), 192)
        copies.append(pltpu.make_async_copy(half_ref.at[pl.ds(k * 192, 192)], o_hbm.at[rows], sem.at[k]))
        copies[-1].start()
    return copies


def place_own_kernel(half_ref, new_ref, o_hbm, new_hbm, sem, new_sem):
    core = lax.rem(lax.axis_index("user"), 2)
    arrive(place(core, half_ref, o_hbm, sem) + fetch(new_ref, new_hbm, new_sem, 4))


def place_other_kernel(half_ref, whole, o_hbm, sem):
    core = lax.rem(lax.axis_index("user"), 2)
    arrive(place(1 - core, half_ref, o_hbm, sem))


def near(value):
    return pltpu.with_memory_space_constraint(value, pltpu.VMEM)


def far(value):
    return pltpu.with_memory_space_constraint(value, pltpu.HBM)


def call(kernel, out_shapes, specs, scratch=(), limit=8, out_specs=VMEM, cost=None, alias={}):
    single = len(out_shapes) == 1
    return pl.pallas_call(
        kernel,
        out_shape=out_shapes[0] if single else out_shapes,
        in_specs=specs,
        out_specs=out_specs if single or isinstance(out_specs, list) else [out_specs] * len(out_shapes),
        scratch_shapes=scratch,
        compiler_params=pltpu.CompilerParams(vmem_limit_bytes=limit << 20),
        cost_estimate=cost,
        input_output_aliases=alias,
    )


def body(ratings, presence, user_factors, item_factors, step_sizes):
    swap = [(k, k ^ 1) for k in range(16)]
    chips = [[k + 2 * j for j in range(8)] for k in range(2)]
    x = call(
        user_kernel,
        [pltpu.VMEM((PIECES, TILES, 4, BLK), F32)],
        [HBM, HBM, HBM, HBM],
        [
            pltpu.SMEM((UB, IB), jnp.int32),
            pltpu.VMEM((USERS, ITEMS), BF16),
            pltpu.VMEM((USERS, BLK), F32),
            pltpu.VMEM((ITEMS, BLK), F32),
            pltpu.VMEM((ITEMS, 2 * BLK), BF16),
            pltpu.VMEM((IB, 2 * BLK, BLK), BF16),
            pltpu.VMEM((IB, BLK, BLK), F32),
            pltpu.VMEM((UB * 64, BLK), F32),
            pltpu.SemaphoreType.DMA((UB,)),
            pltpu.SemaphoreType.DMA((4,)),
            pltpu.SemaphoreType.DMA((2,)),
            pltpu.SemaphoreType.DMA,
        ],
        limit=16,
    )(far(presence), far(ratings), far(user_factors), far(item_factors))
    y = lax.all_to_all(x, "item", 0, 0, tiled=True)
    z, extra = call(
        total_kernel,
        [pltpu.VMEM((PIECES, SENT, BLK), F32), pltpu.VMEM((8, BLK), F32)],
        [VMEM],
        [pltpu.VMEM((SENT + 8, BLK), F32)],
    )(near(y))
    z = lax.all_to_all(z, "item", 0, 0, tiled=True)
    new, other, turned, grams = call(
        item_kernel,
        [
            pltpu.VMEM((USERS, BLK), F32),
            pltpu.VMEM((8, CHUNK + 8, BLK), F32),
            pltpu.VMEM((2 * BLK, USERS), BF16),
            pltpu.VMEM((UB, BLK, BLK), F32),
        ],
        [SMEM, SMEM, VMEM, VMEM, VMEM, VMEM, VMEM],
        limit=16,
    )(presence, step_sizes, near(ratings), near(user_factors), near(item_factors), near(z), near(extra))
    received = lax.ppermute(other, "user", swap)
    own = call(
        own_kernel,
        [pltpu.VMEM((8, CHUNK + 8, BLK), F32)],
        [SMEM, SMEM, VMEM, VMEM, VMEM, VMEM],
        limit=16,
        cost=pl.CostEstimate(flops=1 << 32, bytes_accessed=1 << 23, transcendentals=0),
    )(presence, step_sizes, near(ratings), near(item_factors), near(turned), near(grams))
    v = own + received
    v = lax.all_to_all(v, "user", 0, 0, tiled=True, axis_index_groups=chips)
    owned = call(scale_kernel, [pltpu.VMEM((8, CHUNK, BLK), F32)], [VMEM, VMEM])(
        near(v), near(item_factors)
    )
    mine = lax.all_to_all(owned, "user", 0, 0, tiled=True, axis_index_groups=chips)
    theirs = lax.ppermute(mine, "user", swap)
    half, new_users = call(
        place_own_kernel,
        [pltpu.HBM((ITEMS, BLK), F32), pltpu.HBM((USERS, BLK), F32)],
        [VMEM, VMEM],
        [pltpu.SemaphoreType.DMA((4,)), pltpu.SemaphoreType.DMA((4,))],
        out_specs=HBM,
        cost=pl.CostEstimate(flops=1 << 30, bytes_accessed=1 << 22, transcendentals=0),
    )(near(mine.reshape(ITEMS // 2, BLK)), near(new))
    new_items = call(
        place_other_kernel,
        [pltpu.HBM((ITEMS, BLK), F32)],
        [VMEM, HBM],
        [pltpu.SemaphoreType.DMA((4,))],
        out_specs=HBM,
        alias={1: 0},
    )(near(theirs.reshape(ITEMS // 2, BLK)), half)
    return new_users, new_items


def solution(mesh):
    return jax.shard_map(
        body,
        mesh=mesh,
        in_specs=(P("user", "item"), P("user", "item"), P("user", None), P("item", None), P()),
        out_specs=(P("user", None), P("item", None)),
        check_vma=False,
    )
```

```python
import jax
import jax.numpy as jnp
from jax import lax
from jax.experimental import pallas as pl
from jax.experimental.pallas import tpu as pltpu
from jax.sharding import PartitionSpec as P

BLK = 128
UB = 6
IB = 12
USERS = UB * BLK
ITEMS = IB * BLK
PIECES = 16
ROWS = USERS // PIECES
HROWS = UB * 64 // PIECES
SENT = ROWS + HROWS
TILES = SENT // 4 + 1
CHUNK = ITEMS // 16
F32 = jnp.float32
BF16 = jnp.bfloat16
VMEM = pl.BlockSpec(memory_space=pltpu.VMEM)
SMEM = pl.BlockSpec(memory_space=pltpu.SMEM)
HBM = pl.BlockSpec(memory_space=pltpu.HBM)


def split(value, axis):
    high = value.astype(BF16)
    low = (value - high.astype(F32)).astype(BF16)
    return jnp.concatenate([high, low], axis=axis)


def halves(value):
    return value[:, :BLK] + value[:, BLK:]


def gram(both, turned):
    square = jnp.dot(turned, both, preferred_element_type=F32)
    return halves(square[:BLK] + square[BLK:])


def thirds(value):
    high = value.astype(BF16)
    rest = value - high.astype(F32)
    middle = rest.astype(BF16)
    return high, middle, (rest - middle.astype(F32)).astype(BF16)


def exact(a, b):
    ah, am, al = thirds(a)
    bh, bm, bl = thirds(b)
    left = jnp.concatenate([ah, am, ah, al], axis=1)
    near_zero = jnp.zeros_like(bl)
    right = jnp.concatenate(
        [
            jnp.concatenate([bh, bh, bl, bh], axis=0),
            jnp.concatenate([bm, bm, near_zero, near_zero], axis=0),
        ],
        axis=1,
    )
    return halves(jnp.dot(left, right, preferred_element_type=F32))


def lanes(shape):
    return lax.broadcasted_iota(jnp.int32, shape, 1)


def sublanes(shape):
    return lax.broadcasted_iota(jnp.int32, shape, 0)


def block(index):
    return slice(index * BLK, (index + 1) * BLK)


def present(m_ref, b, j):
    return m_ref[b, j].astype(F32)


def fetch(source, target, sem, parts):
    rows = source.shape[0] // parts
    copies = []
    for k in range(parts):
        part = pl.ds(k * rows, rows)
        copies.append(pltpu.make_async_copy(source.at[part], target.at[part], sem.at[k]))
        copies[-1].start()
    return copies


def arrive(copies):
    for copy in copies:
        copy.wait()


def only_present(m_ref, r_ref, blocks, columns, first, count):
    return jnp.concatenate(
        [
            jnp.concatenate(
                [
                    r_ref[block(b), pl.ds(pl.multiple_of(columns + k * BLK, BLK), BLK)]
                    * present(m_ref, b, first + k).astype(BF16)
                    for k in range(count)
                ],
                axis=1,
            )
            for b in blocks
        ],
        axis=0,
    )


def user_kernel(
    m_hbm, r_hbm, p_hbm, q_hbm, x_ref, m_ref, r_ref, p_ref, q_ref, qcat, turned, grams, packed, r_sem, q_sem, p_sem, m_sem
):
    q_copies = fetch(q_hbm, q_ref, q_sem, 4)
    m_copy = pltpu.make_async_copy(m_hbm, m_ref, m_sem)
    m_copy.start()
    p_copies = fetch(p_hbm, p_ref, p_sem, 2)
    r_copies = fetch(r_hbm, r_ref, r_sem, UB)
    for j in range(IB):
        if j in (0, 3):
            arrive(q_copies[:1] if j == 0 else q_copies[1:])
        q = q_ref[block(j)]
        qcat[block(j)] = split(q, 1)
        turned[j] = split(q.T, 0)
    for j in range(IB):
        grams[j] = gram(qcat[block(j)], turned[j])
    row64, lane64 = sublanes((64, BLK)), lanes((64, BLK))
    extra_row, extra_lane = sublanes((8, BLK)), lanes((8, BLK))
    extra = jnp.zeros((8, BLK), F32)
    arrive([m_copy] + p_copies + r_copies)
    masked = only_present(m_ref, r_ref, range(UB), 0, 0, IB)
    found = halves(jnp.dot(masked, qcat[...], preferred_element_type=F32))
    corrections = []
    for b in range(UB):
        h = jnp.zeros((BLK, BLK), F32)
        count = jnp.int32(0)
        for j in range(IB):
            h = h + present(m_ref, b, j) * grams[j]
            count = count + m_ref[b, j]
        moved = jnp.concatenate([h[64:, 64:], h[64:, :64]], axis=1)
        packed[b * 64 : (b + 1) * 64] = jnp.where((lane64 < 64) & (lane64 > row64), moved, h[:64])
        diagonal = jnp.sum(jnp.where(lane64 == row64 + 64, h[64:], 0.0), axis=0, keepdims=True)
        if b % 2:
            diagonal = jnp.concatenate([diagonal[:, 64:], diagonal[:, :64]], axis=1)
        extra = extra + jnp.where(extra_row == b // 2, jnp.broadcast_to(diagonal, (8, BLK)), 0.0)
        extra = extra + jnp.where((extra_row == 3) & (extra_lane == b), count.astype(F32), 0.0)
        corrections.append(exact(p_ref[block(b)], h))
    d = found - jnp.concatenate(corrections, axis=0)
    for k in range(PIECES * ROWS // 4):
        x_ref[k // 12, k % 12] = d[k * 4 : (k + 1) * 4]
    for piece in range(PIECES):
        for k in range(HROWS // 4):
            x_ref[piece, ROWS // 4 + k] = packed[piece * HROWS + k * 4 : piece * HROWS + (k + 1) * 4]
        x_ref[piece, SENT // 4] = extra[:4]


def total_kernel(y_ref, z_ref, extra_ref, rows):
    for k in range(TILES):
        total = y_ref[0, k]
        for piece in range(1, PIECES):
            total = total + y_ref[piece, k]
        rows[k * 4 : (k + 1) * 4] = total
    extra_ref[...] = rows[SENT : SENT + 8]
    total = rows[:SENT]
    for piece in range(PIECES):
        z_ref[piece] = total


def item_kernel(
    m_ref, step_ref, r_ref, p_ref, q_ref, z_ref, extra_ref, new_ref, other_ref, turned_ref, grams
):
    extra = extra_ref[...]
    scales = step_ref[0] / (BLK * (1.0 + extra[3:4]))
    flipped = jnp.concatenate([extra[:, 64:], extra[:, :64]], axis=1)
    row64, lane64 = sublanes((64, BLK)), lanes((64, BLK))
    for b in range(UB):
        tiles = []
        for k in range(0, BLK, 16):
            piece, at = divmod(b * BLK + k, ROWS)
            tiles.append(z_ref[piece, at : at + 16])
        d = jnp.concatenate(tiles, axis=0)
        tiles = []
        for k in range(0, 64, 8):
            piece, at = divmod(b * 64 + k, HROWS)
            tiles.append(z_ref[piece, ROWS + at : ROWS + at + 8])
        half = jnp.concatenate(tiles, axis=0)
        turned = jnp.concatenate([half[:, 64:], half[:, :64]], axis=1)
        top = jnp.where(lane64 < row64, half, jnp.where(lane64 == row64, 0.5 * half, 0.0))
        top = jnp.where(lane64 >= 64, half, top)
        bottom = jnp.where(lane64 > row64 + 64, turned, 0.0)
        bottom = jnp.where(lane64 == row64 + 64, 0.5 * (flipped if b % 2 else extra)[b // 2 : b // 2 + 1], bottom)
        w = jnp.concatenate([top, bottom], axis=0)
        s = scales[:, b : b + 1]
        new = p_ref[block(b)] + (2.0 * s) * d - (s * s) * exact(d, w + w.T)
        new_ref[block(b)] = new
    for b in range(UB):
        new = new_ref[block(b)]
        turned = split(new.T, 0)
        turned_ref[:, block(b)] = turned
        grams[b] = gram(split(new, 1), turned)
    core = lax.rem(lax.axis_index("user"), 2)
    item_half(1 - core, m_ref, step_ref, r_ref, q_ref, turned_ref, grams, other_ref)


def item_half(side, m_ref, step_ref, r_ref, q_ref, turned_ref, grams, o_ref):
    counts = jnp.zeros((8, BLK), F32)
    row8, lane8 = sublanes((8, BLK)), lanes((8, BLK))
    for j in range(IB):
        count = jnp.int32(0)
        for b in range(UB):
            count = count + m_ref[b, j]
        counts = counts + jnp.where(lane8 == j, count.astype(F32), 0.0)
    step = jnp.where(lax.axis_index("user") == 0, step_ref[1], 0.0)
    counts = jnp.where(row8 == 0, counts, step)
    first = side * (IB // 2)
    columns = pl.multiple_of(side * (ITEMS // 2), BLK)
    masked = only_present(m_ref, r_ref, range(UB), columns, first, IB // 2)
    found = jnp.dot(turned_ref[...], masked, preferred_element_type=F32)
    found = found[:BLK] + found[BLK:]
    for k in range(IB // 2):
        s = jnp.zeros((BLK, BLK), F32)
        for b in range(UB):
            s = s + present(m_ref, b, first + k) * grams[b]
        q = q_ref[pl.ds(pl.multiple_of(columns + k * BLK, BLK), BLK)]
        grad = found[:, block(k)].T - exact(q, s)
        for part in range(4):
            piece, at = divmod(k * 4 + part, 3)
            o_ref[piece, at * 32 : (at + 1) * 32] = grad[part * 32 : (part + 1) * 32]
    for piece in range(8):
        o_ref[piece, CHUNK:] = counts


def own_kernel(m_ref, step_ref, r_ref, q_ref, turned_ref, grams, own_ref):
    core = lax.rem(lax.axis_index("user"), 2)
    item_half(core, m_ref, step_ref, r_ref, q_ref, turned_ref, grams, own_ref)


def scale_kernel(v_ref, q_ref, o_ref):
    user = lax.axis_index("user")
    total = v_ref[0]
    for k in range(1, 8):
        total = total + v_ref[k]
    scales = total[CHUNK + 1 : CHUNK + 2] / (BLK * (1.0 + total[CHUNK : CHUNK + 1]))
    lane1 = lanes((1, BLK))
    for k in range(3):
        place = lax.rem(user, 2) * 24 + (user // 2) * 3 + k
        t = jnp.sum(jnp.where(lane1 == place // 4, scales, 0.0), axis=1, keepdims=True)
        start = pl.multiple_of(place * 32, 8)
        new = q_ref[pl.ds(start, 32)] + t * total[k * 32 : (k + 1) * 32]
        for piece in range(8):
            o_ref[piece, k * 32 : (k + 1) * 32] = new


def place(first, half_ref, o_hbm, sem):
    rows = half_ref.shape[0] // sem.shape[0]
    copies = []
    for k in range(sem.shape[0]):
        target = pl.ds(pl.multiple_of(first + k * rows, 8), rows)
        copies.append(pltpu.make_async_copy(half_ref.at[pl.ds(k * rows, rows)], o_hbm.at[target], sem.at[k]))
        copies[-1].start()
    return copies


def place_own_kernel(half_ref, new_ref, o_hbm, new_hbm, sem, new_sem):
    core = lax.rem(lax.axis_index("user"), 2)
    arrive(place(core * (ITEMS // 2), half_ref, o_hbm, sem) + fetch(new_ref, new_hbm, new_sem, 4))


def place_early_kernel(part_ref, whole, o_hbm, sem):
    core = lax.rem(lax.axis_index("user"), 2)
    arrive(place((1 - core) * (ITEMS // 2), part_ref, o_hbm, sem))


def place_late_kernel(part_ref, whole, o_hbm, sem):
    core = lax.rem(lax.axis_index("user"), 2)
    arrive(place((1 - core) * (ITEMS // 2) + ITEMS // 4, part_ref, o_hbm, sem))


def near(value):
    return pltpu.with_memory_space_constraint(value, pltpu.VMEM)


def far(value):
    return pltpu.with_memory_space_constraint(value, pltpu.HBM)


def call(kernel, out_shapes, specs, scratch=(), limit=8, out_specs=VMEM, cost=None, alias={}):
    single = len(out_shapes) == 1
    return pl.pallas_call(
        kernel,
        out_shape=out_shapes[0] if single else out_shapes,
        in_specs=specs,
        out_specs=out_specs if single or isinstance(out_specs, list) else [out_specs] * len(out_shapes),
        scratch_shapes=scratch,
        compiler_params=pltpu.CompilerParams(vmem_limit_bytes=limit << 20),
        cost_estimate=cost,
        input_output_aliases=alias,
    )


def body(ratings, presence, user_factors, item_factors, step_sizes):
    swap = [(k, k ^ 1) for k in range(16)]
    chips = [[k + 2 * j for j in range(8)] for k in range(2)]
    x = call(
        user_kernel,
        [pltpu.VMEM((PIECES, TILES, 4, BLK), F32)],
        [HBM, HBM, HBM, HBM],
        [
            pltpu.SMEM((UB, IB), jnp.int32),
            pltpu.VMEM((USERS, ITEMS), BF16),
            pltpu.VMEM((USERS, BLK), F32),
            pltpu.VMEM((ITEMS, BLK), F32),
            pltpu.VMEM((ITEMS, 2 * BLK), BF16),
            pltpu.VMEM((IB, 2 * BLK, BLK), BF16),
            pltpu.VMEM((IB, BLK, BLK), F32),
            pltpu.VMEM((UB * 64, BLK), F32),
            pltpu.SemaphoreType.DMA((UB,)),
            pltpu.SemaphoreType.DMA((4,)),
            pltpu.SemaphoreType.DMA((2,)),
            pltpu.SemaphoreType.DMA,
        ],
        limit=16,
    )(far(presence), far(ratings), far(user_factors), far(item_factors))
    y = lax.all_to_all(x, "item", 0, 0, tiled=True)
    z, extra = call(
        total_kernel,
        [pltpu.VMEM((PIECES, SENT, BLK), F32), pltpu.VMEM((8, BLK), F32)],
        [VMEM],
        [pltpu.VMEM((SENT + 8, BLK), F32)],
    )(near(y))
    z = lax.all_to_all(z, "item", 0, 0, tiled=True)
    new, other, turned, grams = call(
        item_kernel,
        [
            pltpu.VMEM((USERS, BLK), F32),
            pltpu.VMEM((8, CHUNK + 8, BLK), F32),
            pltpu.VMEM((2 * BLK, USERS), BF16),
            pltpu.VMEM((UB, BLK, BLK), F32),
        ],
        [SMEM, SMEM, VMEM, VMEM, VMEM, VMEM, VMEM],
        limit=16,
    )(presence, step_sizes, near(ratings), near(user_factors), near(item_factors), near(z), near(extra))
    received = lax.ppermute(other, "user", swap)
    own = call(
        own_kernel,
        [pltpu.VMEM((8, CHUNK + 8, BLK), F32)],
        [SMEM, SMEM, VMEM, VMEM, VMEM, VMEM],
        limit=16,
        cost=pl.CostEstimate(flops=1 << 32, bytes_accessed=1 << 23, transcendentals=0),
    )(presence, step_sizes, near(ratings), near(item_factors), near(turned), near(grams))
    v = own + received
    v = lax.all_to_all(v, "user", 0, 0, tiled=True, axis_index_groups=chips)
    owned = call(scale_kernel, [pltpu.VMEM((8, CHUNK, BLK), F32)], [VMEM, VMEM])(
        near(v), near(item_factors)
    )
    mine = lax.all_to_all(owned, "user", 0, 0, tiled=True, axis_index_groups=chips)
    theirs = [lax.ppermute(mine[k : k + 4], "user", swap) for k in (0, 4)]
    half, new_users = call(
        place_own_kernel,
        [pltpu.HBM((ITEMS, BLK), F32), pltpu.HBM((USERS, BLK), F32)],
        [VMEM, VMEM],
        [pltpu.SemaphoreType.DMA((4,)), pltpu.SemaphoreType.DMA((4,))],
        out_specs=HBM,
        cost=pl.CostEstimate(flops=1 << 30, bytes_accessed=1 << 22, transcendentals=0),
    )(near(mine.reshape(ITEMS // 2, BLK)), near(new))
    for kernel, part in zip((place_early_kernel, place_late_kernel), theirs):
        half = call(
            kernel,
            [pltpu.HBM((ITEMS, BLK), F32)],
            [VMEM, HBM],
            [pltpu.SemaphoreType.DMA((2,))],
            out_specs=HBM,
            cost=pl.CostEstimate(flops=1 << 29, bytes_accessed=1 << 21, transcendentals=0),
            alias={1: 0},
        )(near(part.reshape(ITEMS // 4, BLK)), half)
    new_items = half
    return new_users, new_items


def solution(mesh):
    return jax.shard_map(
        body,
        mesh=mesh,
        in_specs=(P("user", "item"), P("user", "item"), P("user", None), P("item", None), P()),
        out_specs=(P("user", None), P("item", None)),
        check_vma=False,
    )
```

```python
import jax
import jax.numpy as jnp
from jax import lax
from jax.experimental import pallas as pl
from jax.experimental.pallas import tpu as pltpu
from jax.sharding import PartitionSpec as P

BLK = 128
UB = 6
IB = 12
USERS = UB * BLK
ITEMS = IB * BLK
PIECES = 16
ROWS = USERS // PIECES
HROWS = UB * 64 // PIECES
SENT = ROWS + HROWS
TILES = SENT // 4 + 1
CHUNK = ITEMS // 16
F32 = jnp.float32
BF16 = jnp.bfloat16
VMEM = pl.BlockSpec(memory_space=pltpu.VMEM)
SMEM = pl.BlockSpec(memory_space=pltpu.SMEM)
HBM = pl.BlockSpec(memory_space=pltpu.HBM)


def split(value, axis):
    high = value.astype(BF16)
    low = (value - high.astype(F32)).astype(BF16)
    return jnp.concatenate([high, low], axis=axis)


def halves(value):
    return value[:, :BLK] + value[:, BLK:]


def gram(both, turned):
    square = jnp.dot(turned, both, preferred_element_type=F32)
    return halves(square[:BLK] + square[BLK:])


def thirds(value):
    high = value.astype(BF16)
    rest = value - high.astype(F32)
    middle = rest.astype(BF16)
    return high, middle, (rest - middle.astype(F32)).astype(BF16)


def exact(a, b):
    ah, am, al = thirds(a)
    bh, bm, bl = thirds(b)
    left = jnp.concatenate([ah, am, ah, al], axis=1)
    near_zero = jnp.zeros_like(bl)
    right = jnp.concatenate(
        [
            jnp.concatenate([bh, bh, bl, bh], axis=0),
            jnp.concatenate([bm, bm, near_zero, near_zero], axis=0),
        ],
        axis=1,
    )
    return halves(jnp.dot(left, right, preferred_element_type=F32))


def lanes(shape):
    return lax.broadcasted_iota(jnp.int32, shape, 1)


def sublanes(shape):
    return lax.broadcasted_iota(jnp.int32, shape, 0)


def block(index):
    return slice(index * BLK, (index + 1) * BLK)


def present(m_ref, b, j):
    return m_ref[b, j].astype(F32)


def fetch(source, target, sem, parts):
    rows = source.shape[0] // parts
    copies = []
    for k in range(parts):
        part = pl.ds(k * rows, rows)
        copies.append(pltpu.make_async_copy(source.at[part], target.at[part], sem.at[k]))
        copies[-1].start()
    return copies


def arrive(copies):
    for copy in copies:
        copy.wait()


def only_present(m_ref, r_ref, blocks, columns, first, count):
    return jnp.concatenate(
        [
            jnp.concatenate(
                [
                    r_ref[block(b), pl.ds(pl.multiple_of(columns + k * BLK, BLK), BLK)]
                    * present(m_ref, b, first + k).astype(BF16)
                    for k in range(count)
                ],
                axis=1,
            )
            for b in blocks
        ],
        axis=0,
    )


def user_kernel(
    m_hbm, r_hbm, p_hbm, q_hbm, x_ref, m_ref, r_ref, p_ref, q_ref, qcat, turned, grams, packed, r_sem, q_sem, p_sem, m_sem
):
    q_copies = fetch(q_hbm, q_ref, q_sem, 12)
    m_copy = pltpu.make_async_copy(m_hbm, m_ref, m_sem)
    m_copy.start()
    p_copies = fetch(p_hbm, p_ref, p_sem, 2)
    r_copies = fetch(r_hbm, r_ref, r_sem, 2 * UB)
    for j in range(IB):
        if j in (0, 3):
            arrive(q_copies[:3] if j == 0 else q_copies[3:])
        q = q_ref[block(j)]
        qcat[block(j)] = split(q, 1)
        turned[j] = split(q.T, 0)
    for j in range(IB):
        grams[j] = gram(qcat[block(j)], turned[j])
    row64, lane64 = sublanes((64, BLK)), lanes((64, BLK))
    extra_row, extra_lane = sublanes((8, BLK)), lanes((8, BLK))
    extra = jnp.zeros((8, BLK), F32)
    arrive([m_copy] + p_copies + r_copies)
    masked = only_present(m_ref, r_ref, range(UB), 0, 0, IB)
    found = halves(jnp.dot(masked, qcat[...], preferred_element_type=F32))
    corrections = []
    for b in range(UB):
        h = jnp.zeros((BLK, BLK), F32)
        count = jnp.int32(0)
        for j in range(IB):
            h = h + present(m_ref, b, j) * grams[j]
            count = count + m_ref[b, j]
        moved = jnp.concatenate([h[64:, 64:], h[64:, :64]], axis=1)
        packed[b * 64 : (b + 1) * 64] = jnp.where((lane64 < 64) & (lane64 > row64), moved, h[:64])
        diagonal = jnp.sum(jnp.where(lane64 == row64 + 64, h[64:], 0.0), axis=0, keepdims=True)
        if b % 2:
            diagonal = jnp.concatenate([diagonal[:, 64:], diagonal[:, :64]], axis=1)
        extra = extra + jnp.where(extra_row == b // 2, jnp.broadcast_to(diagonal, (8, BLK)), 0.0)
        extra = extra + jnp.where((extra_row == 3) & (extra_lane == b), count.astype(F32), 0.0)
        corrections.append(exact(p_ref[block(b)], h))
    d = found - jnp.concatenate(corrections, axis=0)
    for k in range(PIECES * ROWS // 4):
        x_ref[k // 12, k % 12] = d[k * 4 : (k + 1) * 4]
    for piece in range(PIECES):
        for k in range(HROWS // 4):
            x_ref[piece, ROWS // 4 + k] = packed[piece * HROWS + k * 4 : piece * HROWS + (k + 1) * 4]
        x_ref[piece, SENT // 4] = extra[:4]


def total_kernel(y_ref, z_ref, extra_ref, rows):
    for k in range(TILES):
        total = y_ref[0, k]
        for piece in range(1, PIECES):
            total = total + y_ref[piece, k]
        rows[k * 4 : (k + 1) * 4] = total
    extra_ref[...] = rows[SENT : SENT + 8]
    total = rows[:SENT]
    for piece in range(PIECES):
        z_ref[piece] = total


def item_kernel(
    m_ref, step_ref, r_ref, p_ref, q_ref, z_ref, extra_ref, new_ref, other_ref, turned_ref, grams
):
    extra = extra_ref[...]
    scales = step_ref[0] / (BLK * (1.0 + extra[3:4]))
    flipped = jnp.concatenate([extra[:, 64:], extra[:, :64]], axis=1)
    row64, lane64 = sublanes((64, BLK)), lanes((64, BLK))
    for b in range(UB):
        tiles = []
        for k in range(0, BLK, 16):
            piece, at = divmod(b * BLK + k, ROWS)
            tiles.append(z_ref[piece, at : at + 16])
        d = jnp.concatenate(tiles, axis=0)
        tiles = []
        for k in range(0, 64, 8):
            piece, at = divmod(b * 64 + k, HROWS)
            tiles.append(z_ref[piece, ROWS + at : ROWS + at + 8])
        half = jnp.concatenate(tiles, axis=0)
        turned = jnp.concatenate([half[:, 64:], half[:, :64]], axis=1)
        top = jnp.where(lane64 < row64, half, jnp.where(lane64 == row64, 0.5 * half, 0.0))
        top = jnp.where(lane64 >= 64, half, top)
        bottom = jnp.where(lane64 > row64 + 64, turned, 0.0)
        bottom = jnp.where(lane64 == row64 + 64, 0.5 * (flipped if b % 2 else extra)[b // 2 : b // 2 + 1], bottom)
        w = jnp.concatenate([top, bottom], axis=0)
        s = scales[:, b : b + 1]
        new = p_ref[block(b)] + (2.0 * s) * d - (s * s) * exact(d, w + w.T)
        new_ref[block(b)] = new
    for b in range(UB):
        new = new_ref[block(b)]
        turned = split(new.T, 0)
        turned_ref[:, block(b)] = turned
        grams[b] = gram(split(new, 1), turned)
    core = lax.rem(lax.axis_index("user"), 2)
    item_half(1 - core, m_ref, step_ref, r_ref, q_ref, turned_ref, grams, other_ref)


def item_half(side, m_ref, step_ref, r_ref, q_ref, turned_ref, grams, o_ref):
    counts = jnp.zeros((8, BLK), F32)
    row8, lane8 = sublanes((8, BLK)), lanes((8, BLK))
    for j in range(IB):
        count = jnp.int32(0)
        for b in range(UB):
            count = count + m_ref[b, j]
        counts = counts + jnp.where(lane8 == j, count.astype(F32), 0.0)
    step = jnp.where(lax.axis_index("user") == 0, step_ref[1], 0.0)
    counts = jnp.where(row8 == 0, counts, step)
    first = side * (IB // 2)
    columns = pl.multiple_of(side * (ITEMS // 2), BLK)
    masked = only_present(m_ref, r_ref, range(UB), columns, first, IB // 2)
    found = jnp.dot(turned_ref[...], masked, preferred_element_type=F32)
    found = found[:BLK] + found[BLK:]
    for k in range(IB // 2):
        s = jnp.zeros((BLK, BLK), F32)
        for b in range(UB):
            s = s + present(m_ref, b, first + k) * grams[b]
        q = q_ref[pl.ds(pl.multiple_of(columns + k * BLK, BLK), BLK)]
        grad = found[:, block(k)].T - exact(q, s)
        for part in range(4):
            piece, at = divmod(k * 4 + part, 3)
            o_ref[piece, at * 32 : (at + 1) * 32] = grad[part * 32 : (part + 1) * 32]
    for piece in range(8):
        o_ref[piece, CHUNK:] = counts


def own_kernel(m_ref, step_ref, r_ref, q_ref, turned_ref, grams, own_ref):
    core = lax.rem(lax.axis_index("user"), 2)
    item_half(core, m_ref, step_ref, r_ref, q_ref, turned_ref, grams, own_ref)


def scale_kernel(v_ref, q_ref, o_ref):
    user = lax.axis_index("user")
    total = v_ref[0]
    for k in range(1, 8):
        total = total + v_ref[k]
    scales = total[CHUNK + 1 : CHUNK + 2] / (BLK * (1.0 + total[CHUNK : CHUNK + 1]))
    lane1 = lanes((1, BLK))
    for k in range(3):
        place = lax.rem(user, 2) * 24 + (user // 2) * 3 + k
        t = jnp.sum(jnp.where(lane1 == place // 4, scales, 0.0), axis=1, keepdims=True)
        start = pl.multiple_of(place * 32, 8)
        new = q_ref[pl.ds(start, 32)] + t * total[k * 32 : (k + 1) * 32]
        for piece in range(8):
            o_ref[piece, k * 32 : (k + 1) * 32] = new


def place(side, half_ref, o_hbm, sem):
    copies = []
    for k in range(4):
        rows = pl.ds(pl.multiple_of(side * (ITEMS // 2) + k * 192, 8), 192)
        copies.append(pltpu.make_async_copy(half_ref.at[pl.ds(k * 192, 192)], o_hbm.at[rows], sem.at[k]))
        copies[-1].start()
    return copies


def place_own_kernel(half_ref, new_ref, o_hbm, new_hbm, sem, new_sem):
    core = lax.rem(lax.axis_index("user"), 2)
    arrive(place(core, half_ref, o_hbm, sem) + fetch(new_ref, new_hbm, new_sem, 4))


def place_other_kernel(half_ref, whole, o_hbm, sem):
    core = lax.rem(lax.axis_index("user"), 2)
    arrive(place(1 - core, half_ref, o_hbm, sem))


def near(value):
    return pltpu.with_memory_space_constraint(value, pltpu.VMEM)


def far(value):
    return pltpu.with_memory_space_constraint(value, pltpu.HBM)


def call(kernel, out_shapes, specs, scratch=(), limit=8, out_specs=VMEM, cost=None, alias={}):
    single = len(out_shapes) == 1
    return pl.pallas_call(
        kernel,
        out_shape=out_shapes[0] if single else out_shapes,
        in_specs=specs,
        out_specs=out_specs if single or isinstance(out_specs, list) else [out_specs] * len(out_shapes),
        scratch_shapes=scratch,
        compiler_params=pltpu.CompilerParams(vmem_limit_bytes=limit << 20),
        cost_estimate=cost,
        input_output_aliases=alias,
    )


def body(ratings, presence, user_factors, item_factors, step_sizes):
    swap = [(k, k ^ 1) for k in range(16)]
    chips = [[k + 2 * j for j in range(8)] for k in range(2)]
    x = call(
        user_kernel,
        [pltpu.VMEM((PIECES, TILES, 4, BLK), F32)],
        [HBM, HBM, HBM, HBM],
        [
            pltpu.SMEM((UB, IB), jnp.int32),
            pltpu.VMEM((USERS, ITEMS), BF16),
            pltpu.VMEM((USERS, BLK), F32),
            pltpu.VMEM((ITEMS, BLK), F32),
            pltpu.VMEM((ITEMS, 2 * BLK), BF16),
            pltpu.VMEM((IB, 2 * BLK, BLK), BF16),
            pltpu.VMEM((IB, BLK, BLK), F32),
            pltpu.VMEM((UB * 64, BLK), F32),
            pltpu.SemaphoreType.DMA((2 * UB,)),
            pltpu.SemaphoreType.DMA((12,)),
            pltpu.SemaphoreType.DMA((2,)),
            pltpu.SemaphoreType.DMA,
        ],
        limit=16,
    )(far(presence), far(ratings), far(user_factors), far(item_factors))
    y = lax.all_to_all(x, "item", 0, 0, tiled=True)
    z, extra = call(
        total_kernel,
        [pltpu.VMEM((PIECES, SENT, BLK), F32), pltpu.VMEM((8, BLK), F32)],
        [VMEM],
        [pltpu.VMEM((SENT + 8, BLK), F32)],
    )(near(y))
    z = lax.all_to_all(z, "item", 0, 0, tiled=True)
    new, other, turned, grams = call(
        item_kernel,
        [
            pltpu.VMEM((USERS, BLK), F32),
            pltpu.VMEM((8, CHUNK + 8, BLK), F32),
            pltpu.VMEM((2 * BLK, USERS), BF16),
            pltpu.VMEM((UB, BLK, BLK), F32),
        ],
        [SMEM, SMEM, VMEM, VMEM, VMEM, VMEM, VMEM],
        limit=16,
    )(presence, step_sizes, near(ratings), near(user_factors), near(item_factors), near(z), near(extra))
    received = lax.ppermute(other, "user", swap)
    own = call(
        own_kernel,
        [pltpu.VMEM((8, CHUNK + 8, BLK), F32)],
        [SMEM, SMEM, VMEM, VMEM, VMEM, VMEM],
        limit=16,
        cost=pl.CostEstimate(flops=1 << 32, bytes_accessed=1 << 23, transcendentals=0),
    )(presence, step_sizes, near(ratings), near(item_factors), near(turned), near(grams))
    v = own + received
    v = lax.all_to_all(v, "user", 0, 0, tiled=True, axis_index_groups=chips)
    owned = call(scale_kernel, [pltpu.VMEM((8, CHUNK, BLK), F32)], [VMEM, VMEM])(
        near(v), near(item_factors)
    )
    mine = lax.all_to_all(owned, "user", 0, 0, tiled=True, axis_index_groups=chips)
    theirs = lax.ppermute(mine, "user", swap)
    half, new_users = call(
        place_own_kernel,
        [pltpu.HBM((ITEMS, BLK), F32), pltpu.HBM((USERS, BLK), F32)],
        [VMEM, VMEM],
        [pltpu.SemaphoreType.DMA((4,)), pltpu.SemaphoreType.DMA((4,))],
        out_specs=HBM,
        cost=pl.CostEstimate(flops=1 << 30, bytes_accessed=1 << 22, transcendentals=0),
    )(near(mine.reshape(ITEMS // 2, BLK)), near(new))
    new_items = call(
        place_other_kernel,
        [pltpu.HBM((ITEMS, BLK), F32)],
        [VMEM, HBM],
        [pltpu.SemaphoreType.DMA((4,))],
        out_specs=HBM,
        alias={1: 0},
    )(near(theirs.reshape(ITEMS // 2, BLK)), half)
    return new_users, new_items


def solution(mesh):
    return jax.shard_map(
        body,
        mesh=mesh,
        in_specs=(P("user", "item"), P("user", "item"), P("user", None), P("item", None), P()),
        out_specs=(P("user", None), P("item", None)),
        check_vma=False,
    )
```
